32 devices in a mesh: groups: 2 (over x), dev: 8 (over z, y), sub: 2 (over core).
Axes of the slice: x: 2, y: 2, z: 4, core: 2. Of those that a mesh axis runs over, the one named last changes fastest.
Arguments:
- hidden: bfloat16 [128, 6144], P(('groups', 'dev')), parts along dimension 0, may hold values from -6 to 6
- query: bfloat16 [128, 48, 128], P(('groups', 'dev'), 'sub'), parts along dimension 0, may hold values from -180 to 180
- cache_keys: bfloat16 [128, 8, 64, 128], P(('groups', 'dev'), 'sub'), parts along dimension 0, may hold values from -6 to 6
- cache_values: bfloat16 [128, 8, 64, 128], P(('groups', 'dev'), 'sub'), parts along dimension 0, may hold values from -6 to 6
- lengths: int32 [128], P(('groups', 'dev')), parts along dimension 0, may hold values from 16 to 64
- out_proj: bfloat16 [6144, 6144], P('sub', 'dev'), may hold values from -0.078125 to 0.078125
- norm_gain: float32 [6144], replicated, may hold values from 0.1 to 1.9
- router: bfloat16 [6144, 4], replicated, may hold values from -0.078125 to 0.078125
- low_factor: bfloat16 [6144, 256], P('sub'), may hold values from -0.078125 to 0.078125
- gate_weight: bfloat16 [6144, 32768], P(None, ('dev', 'sub')), may hold values from -0.078125 to 0.078125
- up_weight: bfloat16 [6144, 32768], P(None, ('dev', 'sub')), may hold values from -0.078125 to 0.078125
- down_weight: bfloat16 [32768, 6144], P(('dev', 'sub')), may hold values from -0.0625 to 0.0625
- gate_low: bfloat16 [256, 32768], P(None, ('dev', 'sub')), may hold values from -0.375 to 0.375
- up_low: bfloat16 [256, 32768], P(None, ('dev', 'sub')), may hold values from -0.375 to 0.375
- experts: int32 [128, 2], P(('groups', 'dev')), parts along dimension 0, may hold values from 0 to 3, all different within a row; in each aligned block of 8 rows (0 to 7, 8 to 15, ...) at most 6 rows name the same one
Outputs:
- layer_out: bfloat16 [128, 6144], P(('groups', 'dev')), parts along dimension 0
- mixture: float32 [128, 6144], P(('groups', 'dev')), parts along dimension 0
The draws below stay inside these ranges and needn't reach their ends.
There are 2 independent parts, one for each index of `groups`. The reference program is written for one: setup_inputs(seed, part) draws one part's arguments, and reference() takes and returns one part's arrays. A program takes and returns all parts, laid end to end along the dimension named above; an argument that names none is the same for every part. Nothing has to cross between parts.
Inputs may be any that keep to these rules, and one draw needn't show every extreme that they name: Each row names two different experts. Among the 8 requests of one device no expert is named more than 6 times, and that bound is reached on some device.
All inputs are finite; a program needn't handle non-finite values.
Results may differ from the reference program's by a relative error of at most 0.015.
Values may be sent and summed in bfloat16 or wider, within the bound.
A program may use at most 128 MiB of HBM per device.

```python
import math
import jax
import jax.numpy as jnp
import numpy as np
from jax import lax

D = 6144
QH = 48
KVH = 8
HD = 128
EXPERTS = 4
FF = 8192
RANK = 256
REQ_DEV = 8
SPAN = 64
CAP = 6
REQ = 64


def drawn_pair(key):
    streams = jax.random.split(jax.random.fold_in(key, 31), 2)
    query_draw = jnp.clip(jax.random.normal(streams[0], (REQ, QH, HD), jnp.float32), -6.0, 6.0)
    key_draw = jnp.clip(jax.random.normal(streams[1], (REQ, KVH, SPAN, HD), jnp.float32), -6.0, 6.0)
    return (query_draw, key_draw)


def draw_query(key, part):
    return drawn_pair(key)[0].astype(jnp.bfloat16)


def draw_cache_keys(key, part):
    return drawn_pair(key)[1].astype(jnp.bfloat16)


def set_ends(array, key, least, high):
    spot = [jax.random.randint(jax.random.fold_in(key, axis), (), 0, length) for axis, length in enumerate(array.shape)]
    main_axis = array.shape.index(max(array.shape))
    next_to = spot[:main_axis] + [(spot[main_axis] + 1) % array.shape[main_axis]] + spot[main_axis + 1:]
    return array.at[tuple(spot)].set(least).at[tuple(next_to)].set(high)


def levels(rng, shape, cuts, smallest, top_value):
    def one(axis_at, shards_of):
        draws = jax.random.uniform(jax.random.fold_in(jax.random.fold_in(rng, 6), axis_at), (shards_of,), jnp.float32, smallest / len(cuts), top_value / len(cuts))
        return jnp.repeat(jnp.exp(draws), shape[axis_at] // shards_of).reshape((-1,) + (1,) * (len(shape) - axis_at - 1))

    loudness = one(*cuts[0])
    for cut in cuts[1:]:
        loudness = loudness * one(*cut)
    return loudness


def assign_block(key, own, number, rows, amount, top, most, slope):
    sequence = jax.random.permutation(key, amount)
    heavy_load, usual = portions_of(amount, rows * top, most, slope, True), portions_of(amount, rows * top, most, slope, False)
    places = jnp.arange(amount)

    def named(sizes, offset_by):
        used = int((sizes > 0).sum())
        fixed = max(1, used // 4)
        shifted = fixed + (places - fixed + offset_by * (used - fixed)) % max(1, amount - fixed)
        return jnp.zeros((amount,), jnp.int32).at[sequence[jnp.where(places < fixed, places, shifted)]].set(jnp.asarray(sizes, jnp.int32))

    sizes = jnp.where(number % 4 == 0, named(heavy_load, number // 4), named(usual, number - number // 4 - 1))
    mixed = jax.random.permutation(jax.random.fold_in(own, 3), amount)
    source_of, sink = mixed[0:amount // 2 * 2:2], mixed[1:amount // 2 * 2:2]
    room = jnp.minimum(sizes[source_of] - 1, most - sizes[sink]) // 2
    room = jnp.where((source_of == sequence[0]) | (sink == sequence[0]) | (sizes[sink] == 0), 0, jnp.maximum(room, 0))
    shifted = jax.random.randint(jax.random.fold_in(own, 4), (amount // 2,), 0, 1 << 20) % (room + 1)
    sizes = sizes.at[source_of].add(-shifted).at[sink].add(shifted)
    items = jnp.searchsorted(jnp.cumsum(sizes), jnp.arange(rows * top), side="right").astype(jnp.int32)
    table = items.reshape(top, rows).T
    table = table[jax.random.permutation(jax.random.fold_in(own, 1), rows)]
    offset_by = jax.random.randint(jax.random.fold_in(own, 2), (rows, 1), 0, top)
    return jnp.take_along_axis(table, (jnp.arange(top)[None, :] + offset_by) % top, axis=1)


def portions_of(count, total, limit, skew, full):
    portions = [(1 << 20) // math.isqrt(rank ** skew) + 1 for rank in range(1, count + 1)]
    largest = limit if full else min(limit, max(-(-total // count), total * portions[0] // sum(portions)))
    least = 1 if total - largest >= count - 1 else 0
    holding, surplus = [largest] + [least] * (count - 1), total - largest - least * (count - 1)
    while surplus > 0:
        free = [i for i in range(1, count) if holding[i] < largest] or [i for i in range(1, count) if holding[i] < limit]
        pool, budget = sum([portions[i] for i in free]), surplus
        for i in free:
            extra = min(limit - holding[i], max(1, budget * portions[i] // pool), surplus)
            holding[i] = holding[i] + extra
            surplus = surplus - extra
    return np.array(holding)


def scatter_about(rng, shape, scale, reach, cuts=(), kind=jnp.bfloat16):
    array = jax.random.normal(rng, shape, jnp.float32) * scale
    if len(cuts) > 0:
        array = levels(rng, shape, cuts, -0.22, 0.18) * array
    return jnp.clip(array, min=-reach, max=reach).astype(kind)


def setup_inputs(seed: int = 0, part: int = 0) -> dict:
    arg_keys = jax.random.split(jax.random.key(seed), 16)
    part_keys = jax.random.split(jax.random.fold_in(arg_keys[15], part), 16)
    hidden = scatter_about(part_keys[0], (REQ, D), 1.0, 6.0, ((0, 8),))
    query = draw_query(jax.random.fold_in(jax.random.fold_in(arg_keys[15], part), 71), part)
    cache_keys = draw_cache_keys(jax.random.fold_in(jax.random.fold_in(arg_keys[15], part), 71), part)
    cache_values = scatter_about(part_keys[3], (REQ, KVH, SPAN, HD), 1.0, 6.0, ((0, 8), (1, 2)))
    lengths = set_ends(jax.random.randint(part_keys[4], (REQ,), SPAN // 4, SPAN + 1), jax.random.fold_in(part_keys[4], 1), SPAN // 4, SPAN).astype(jnp.int32)
    out_proj = scatter_about(arg_keys[5], (QH * HD, D), (QH * HD) ** -0.5, 0.078125, ((0, 2), (1, 8)))
    norm_gain = jnp.clip(1.0 + 0.18 * jax.random.normal(arg_keys[6], (D,), jnp.float32), 0.1, 1.9)
    router = scatter_about(arg_keys[7], (D, EXPERTS), D ** -0.5, 0.078125)
    low_factor = scatter_about(arg_keys[8], (D, RANK), D ** -0.5, 0.078125, ((0, 2),))
    gate_weight = scatter_about(arg_keys[9], (D, EXPERTS * FF), D ** -0.5, 0.078125, ((1, 16),))
    up_weight = scatter_about(arg_keys[10], (D, EXPERTS * FF), D ** -0.5, 0.078125, ((1, 16),))
    down_weight = scatter_about(arg_keys[11], (EXPERTS * FF, D), FF ** -0.5, 0.0625, ((0, 16),))
    gate_low = scatter_about(arg_keys[12], (RANK, EXPERTS * FF), RANK ** -0.5, 0.375, ((1, 16),))
    up_low = scatter_about(arg_keys[13], (RANK, EXPERTS * FF), RANK ** -0.5, 0.375, ((1, 16),))
    experts_keys = jax.random.split(jax.random.fold_in(part_keys[14], 1), REQ // REQ_DEV)
    experts_turns = jax.random.permutation(jax.random.fold_in(part_keys[14], 3), REQ // REQ_DEV)
    experts = jax.vmap(lambda own, number: assign_block(jax.random.fold_in(part_keys[14], 2), own, number, REQ_DEV, EXPERTS, 2, CAP, 2))(experts_keys, experts_turns).reshape((REQ, 2))
    return dict(hidden=hidden, query=query, cache_keys=cache_keys, cache_values=cache_values, lengths=lengths, out_proj=out_proj, norm_gain=norm_gain, router=router, low_factor=low_factor, gate_weight=gate_weight, up_weight=up_weight, down_weight=down_weight, gate_low=gate_low, up_low=up_low, experts=experts)


EPSILON = 1e-05

def expert_shard(row_block, low_rank, gate_weight, up_weight, down_weight, gate_low, up_low):
    gate_sum = jnp.dot(row_block, gate_weight, preferred_element_type=jnp.float32) + jnp.dot(low_rank, gate_low, preferred_element_type=jnp.float32)
    up_sum = jnp.dot(row_block, up_weight, preferred_element_type=jnp.float32) + jnp.dot(low_rank, up_low, preferred_element_type=jnp.float32)
    inner_act = (jax.nn.silu(gate_sum) * up_sum).astype(jnp.bfloat16)
    return jnp.dot(inner_act, down_weight, preferred_element_type=jnp.float32)

def route_gates(normed, router, experts):
    logits = jnp.dot(normed, router, preferred_element_type=jnp.float32)
    labels = lax.broadcasted_iota(jnp.int32, (1, 1, router.shape[1]), 2)
    picked = (experts[:, :, None] == labels).astype(jnp.float32)
    chosen = lax.optimization_barrier(jnp.sum(logits[:, None, :] * picked, axis=-1))
    leading = jax.nn.sigmoid(chosen[:, 0] - chosen[:, 1])
    return jnp.stack([leading, 1.0 - leading], axis=-1)

def reference(hidden, query, cache_keys, cache_values, lengths, out_proj, norm_gain, router, low_factor, gate_weight, up_weight, down_weight, gate_low, up_low, experts):
    heads_per_kv = QH // KVH
    grouped = query.astype(jnp.float32).reshape(REQ, KVH, heads_per_kv, HD)
    scores = jnp.einsum('rkgd,rkld->rkgl', grouped, cache_keys.astype(jnp.float32)) * HD ** (-0.5)
    visible = lax.broadcasted_iota(jnp.int32, (REQ, SPAN), 1) < lengths[:, None]
    scores = jnp.where(visible[:, None, None, :], scores, -1e+30)
    attn_probs = jax.nn.softmax(scores, axis=-1).astype(jnp.bfloat16)
    attended = jnp.einsum('rkgl,rkld->rkgd', attn_probs.astype(jnp.float32), cache_values.astype(jnp.float32))
    attended = attended.astype(jnp.bfloat16).reshape(REQ, QH * HD)
    residual = hidden.astype(jnp.float32) + jnp.dot(attended, out_proj, preferred_element_type=jnp.float32)
    inverse = lax.rsqrt(lax.optimization_barrier(jnp.mean(residual * residual, axis=-1, keepdims=True)) + EPSILON)
    normed = (residual * inverse * norm_gain).astype(jnp.bfloat16)
    low_rank = jnp.dot(normed, low_factor, preferred_element_type=jnp.float32).astype(jnp.bfloat16)
    gate_pair = route_gates(normed, router, experts)
    mixture = jnp.zeros((REQ, D), jnp.float32)
    for expert in range(EXPERTS):
        columns = slice(expert * FF, (expert + 1) * FF)
        output = expert_shard(normed, low_rank, gate_weight[:, columns], up_weight[:, columns], down_weight[columns, :], gate_low[:, columns], up_low[:, columns])
        route_share = lax.optimization_barrier(jnp.sum(gate_pair * (experts == expert).astype(jnp.float32), axis=-1))
        mixture = mixture + route_share[:, None] * output
    return ((residual + mixture).astype(jnp.bfloat16), mixture)
```

```python
import functools

import jax
import jax.numpy as jnp
from jax import lax
from jax.experimental import pallas as pl
from jax.experimental.pallas import tpu as pltpu
from jax.sharding import PartitionSpec as P

CAP = 6


EPSILON = 1e-05


def expert_shard(row_block, low_rank, gate_weight, up_weight, down_weight, gate_low, up_low):
    gate_sum = jnp.dot(row_block, gate_weight, preferred_element_type=jnp.float32) + jnp.dot(
        low_rank, gate_low, preferred_element_type=jnp.float32
    )
    up_sum = jnp.dot(row_block, up_weight, preferred_element_type=jnp.float32) + jnp.dot(
        low_rank, up_low, preferred_element_type=jnp.float32
    )
    inner_act = (jax.nn.silu(gate_sum) * up_sum).astype(jnp.bfloat16)
    return jnp.dot(inner_act, down_weight, preferred_element_type=jnp.float32)


def route_gates(normed, router, experts):
    logits = jnp.dot(normed, router, preferred_element_type=jnp.float32)
    labels = lax.broadcasted_iota(jnp.int32, (1, 1, router.shape[1]), 2)
    picked = (experts[:, :, None] == labels).astype(jnp.float32)
    chosen = jnp.sum(logits[:, None, :] * picked, axis=-1)
    leading = jax.nn.sigmoid(chosen[:, 0] - chosen[:, 1])
    return jnp.stack([leading, 1.0 - leading], axis=-1)


def plain_body(
    hidden,
    query,
    cache_keys,
    cache_values,
    lengths,
    out_proj,
    norm_gain,
    router,
    low_factor,
    gate_weight,
    up_weight,
    down_weight,
    gate_low,
    up_low,
    experts,
):
    requests = hidden.shape[0]
    model_width = hidden.shape[1]
    heads_here = query.shape[1]
    kv_here = cache_keys.shape[1]
    span_len = cache_keys.shape[2]
    head_size = query.shape[2]
    grouped = query.reshape(requests, kv_here, heads_here // kv_here, head_size)
    scores = jnp.einsum(
        "rkgd,rkld->rkgl", grouped, cache_keys, preferred_element_type=jnp.float32
    ) * head_size ** (-0.5)
    visible = lax.broadcasted_iota(jnp.int32, (requests, span_len), 1) < lengths[:, None]
    scores = jnp.where(visible[:, None, None, :], scores, -1e30)
    attn_probs = jax.nn.softmax(scores, axis=-1).astype(jnp.bfloat16)
    attended = jnp.einsum(
        "rkgl,rkld->rkgd", attn_probs, cache_values, preferred_element_type=jnp.float32
    )
    attended = attended.astype(jnp.bfloat16).reshape(requests, heads_here * head_size)
    columns = jnp.dot(
        lax.all_gather(attended, "dev", axis=0, tiled=True),
        out_proj,
        preferred_element_type=jnp.float32,
    )
    partial_proj = lax.all_to_all(columns, "dev", split_axis=0, concat_axis=1, tiled=True)
    residual = hidden.astype(jnp.float32) + lax.psum(partial_proj, "sub")
    inverse = lax.rsqrt(jnp.mean(residual * residual, axis=-1, keepdims=True) + EPSILON)
    normed = (residual * inverse * norm_gain).astype(jnp.bfloat16)
    half_width = low_factor.shape[0]
    normed_half = lax.dynamic_slice_in_dim(
        normed, lax.axis_index("sub") * half_width, half_width, 1
    )
    low_partial = jnp.dot(normed_half, low_factor, preferred_element_type=jnp.float32)
    low_rank = lax.psum(low_partial, "sub").astype(jnp.bfloat16)
    rank_width = low_rank.shape[1]
    expert_count = router.shape[1]
    holders = lax.axis_size("dev") // expert_count
    gate_pair = route_gates(normed, router, experts)
    flat_ids = experts.reshape(-1)
    entries = flat_ids.shape[0]
    same_expert = flat_ids[:, None] == flat_ids[None, :]
    earlier = lax.broadcasted_iota(jnp.int32, (entries, entries), 0) > lax.broadcasted_iota(
        jnp.int32, (entries, entries), 1
    )
    slot_index = jnp.sum((same_expert & earlier).astype(jnp.int32), axis=1).reshape(requests, 2)
    target = experts * CAP + slot_index
    placement = (
        target[:, :, None] == lax.broadcasted_iota(jnp.int32, (1, 1, expert_count * CAP), 2)
    ).astype(jnp.float32)
    chosen = jnp.sum(placement, axis=1).astype(jnp.bfloat16)
    packed_rows = jnp.einsum(
        "rs,rd->sd", chosen, normed, preferred_element_type=jnp.float32
    ).astype(jnp.bfloat16)
    packed_low = jnp.einsum(
        "rs,rd->sd", chosen, low_rank, preferred_element_type=jnp.float32
    ).astype(jnp.bfloat16)
    send_rows = jnp.repeat(packed_rows.reshape(expert_count, CAP, model_width), holders, axis=0)
    send_low = jnp.repeat(packed_low.reshape(expert_count, CAP, rank_width), holders, axis=0)
    got_rows = lax.all_to_all(send_rows, "dev", split_axis=0, concat_axis=0, tiled=True)
    got_low = lax.all_to_all(send_low, "dev", split_axis=0, concat_axis=0, tiled=True)
    sources = got_rows.shape[0]
    slot_count = got_rows.shape[1]
    result = expert_shard(
        got_rows.reshape(sources * slot_count, model_width),
        got_low.reshape(sources * slot_count, rank_width),
        gate_weight,
        up_weight,
        down_weight,
        gate_low,
        up_low,
    )
    partials = result.reshape(sources, slot_count, model_width)
    returned = lax.all_to_all(
        partials.astype(jnp.bfloat16), "dev", split_axis=0, concat_axis=0, tiled=True
    ).astype(partials.dtype)
    per_slot = jnp.sum(returned.reshape(expert_count, holders, CAP, model_width), axis=1).reshape(
        expert_count * CAP, model_width
    )
    weighted = jnp.sum(placement * gate_pair[:, :, None], axis=1)
    mixture_part = jnp.dot(weighted, per_slot, precision=lax.Precision.HIGHEST)
    mixture = lax.psum(mixture_part.astype(jnp.bfloat16), "sub").astype(jnp.float32)
    return ((residual + mixture).astype(jnp.bfloat16), mixture)


CHUNK = 512
NEAR = 2
FAR_ORDER = (2, 3, 1)
FAR_STEPS = (1, 3, 2)
FAR_AT = (2, 3, 4)
RELAYED_AT = (7, 8, 9)
GATE_SLOTS = 11
DOWN_SLOTS = 6
VMEM_BYTES = 66 * 10**6
F32 = jnp.float32
BF16 = jnp.bfloat16


def layer_kernel(
    devs,
    subs,
    gate_slots,
    down_slots,
    hidden,
    query,
    keys,
    values,
    lengths,
    out_proj,
    gain,
    router,
    low_factor,
    gate_w,
    up_w,
    down_w,
    gate_low,
    up_low,
    experts,
    residual,
    mixture,
    ring_a,
    ring_b,
    hid_v,
    q_v,
    k_v,
    v_v,
    op_v,
    lf_v,
    gl_v,
    ul_v,
    att_h,
    att_all,
    hid_all,
    pair_send,
    pair_recv,
    res_all,
    x_v,
    sq_v,
    low_v,
    logit_v,
    acc,
    inner,
    dsend,
    drecv,
    rsend,
    rrecv,
    load_sem,
    a_sem,
    b_sem,
    csend_sem,
    crecv_sem,
    asend_sem,
    arecv_sem,
    gsend_sem,
    grecv_sem,
    fsend_sem,
    frecv_sem,
    psend_sem,
    precv_sem,
    xsend_sem,
    xrecv_sem,
    rs_sem,
    rr_sem,
    msend_sem,
    mrecv_sem,
):
    me = lax.axis_index("dev")
    s = lax.axis_index("sub")
    mate = 1 - s
    rows, width = hidden.shape
    all_rows = devs * rows
    heads = query.shape[1]
    kv_here, span, hd = keys.shape[1:]
    per_kv = heads // kv_here
    att_width = heads * hd
    cols = out_proj.shape[1]
    part = cols // subs
    units = gate_w.shape[1]
    half = low_factor.shape[0]
    steps = width // (2 * CHUNK)
    gate_chunks = 2 * devs
    down_chunks = 2 * steps

    far = devs // NEAR
    z = me // NEAR
    y = lax.rem(me, NEAR)
    beside = me + 1 - 2 * y

    def far_z(k):
        if k == 1:
            return z + 1 - 2 * lax.rem(z, 2)
        if k == 2:
            return lax.rem(z + 2, far)
        return far - 1 - z

    def far_peer(k):
        return far_z(k) * NEAR + y

    def far_beside(k):
        return far_z(k) * NEAR + 1 - y

    def peer(k):
        return lax.rem(me + k, devs)

    def remote(src, dst, send_sem, recv_sem, d, sub):
        return pltpu.make_async_remote_copy(
            src_ref=src,
            dst_ref=dst,
            send_sem=send_sem,
            recv_sem=recv_sem,
            device_id={"dev": d, "sub": sub},
            device_id_type=pl.DeviceIdType.MESH,
        )

    barrier = pltpu.get_barrier_semaphore()
    for k in range(1, devs):
        pl.semaphore_signal(
            barrier, inc=1, device_id={"dev": peer(k), "sub": s}, device_id_type=pl.DeviceIdType.MESH
        )
    pl.semaphore_signal(
        barrier, inc=1, device_id={"dev": me, "sub": mate}, device_id_type=pl.DeviceIdType.MESH
    )

    loads = [
        pltpu.make_async_copy(src, dst, load_sem.at[n])
        for n, (src, dst) in enumerate(
            [
                (query, q_v),
                (keys, k_v),
                (values, v_v),
                (hidden, hid_v),
                (low_factor, lf_v.at[s]),
                (out_proj, op_v),
                (gate_low, gl_v),
                (up_low, ul_v),
            ]
        )
    ]
    for load in loads:
        load.start()

    def block_at(k):
        kz = jnp.where(k < 2, 0, lax.rem(k - 2, far - 1) + 1)
        beside_too = jnp.where(k < 2, k, jnp.where(k < far + 1, 0, 1))
        zz = z
        for n, f in enumerate(FAR_STEPS):
            zz = jnp.where(kz == n + 1, far_z(f), zz)
        return zz * NEAR + lax.rem(y + beside_too, NEAR)

    def start_a(i):
        slot = lax.rem(i, gate_slots)
        at_rows = pl.ds(pl.multiple_of(block_at(i // 2) * cols, cols), cols)

        @pl.when(lax.rem(i, 2) == 0)
        def _():
            pltpu.make_async_copy(gate_w.at[at_rows], ring_a.at[slot], a_sem.at[slot]).start()

        @pl.when(lax.rem(i, 2) == 1)
        def _():
            pltpu.make_async_copy(up_w.at[at_rows], ring_a.at[slot], a_sem.at[slot]).start()

    def start_b(i):
        slot = lax.rem(i, down_slots)
        for_mate = (i == 0) | ((lax.rem(i, 2) == 1) & (i < down_chunks - 1))
        pair = jnp.where(for_mate, (i + 1) // 2, (i - 1) // 2)
        col = pl.multiple_of((2 * pair + jnp.where(for_mate, mate, s)) * CHUNK, CHUNK)
        pltpu.make_async_copy(
            down_w.at[:, pl.ds(col, CHUNK)], ring_b.at[slot], b_sem.at[slot]
        ).start()

    def loop_start(start):
        def go(i, carry):
            start(i)
            return carry

        return go

    lax.fori_loop(0, gate_slots, loop_start(start_a), 0)
    lax.fori_loop(0, down_slots, loop_start(start_b), 0)

    lane = lax.broadcasted_iota(jnp.int32, (rows, 128), 1)
    row = lax.broadcasted_iota(jnp.int32, (rows, 128), 0)
    named = jnp.zeros((rows, 128), jnp.int32)
    for r in range(rows):
        named = jnp.where(row == r, jnp.where(lane == 0, experts[0, r], experts[1, r]), named)
    att_all[me, :, att_width:] = named.astype(F32).astype(BF16)

    for load in loads[:3]:
        load.wait()
    at = lax.broadcasted_iota(jnp.int32, (heads, kv_here * span), 1)
    head = lax.broadcasted_iota(jnp.int32, (heads, kv_here * span), 0)
    own = (at // span) == (head // per_kv)
    position = at % span
    for r in range(rows):
        scores = (
            lax.dot_general(
                q_v[r],
                k_v[r].reshape(kv_here * span, hd),
                (((1,), (1,)), ((), ())),
                preferred_element_type=F32,
            )
            * hd ** (-0.5)
        )
        scores = jnp.where(own & (position < lengths[r]), scores, -1e30)
        top = jnp.max(scores, axis=-1, keepdims=True)
        e = jnp.exp(scores - top)
        probs = (e / jnp.sum(e, axis=-1, keepdims=True)).astype(BF16)
        att_h[:, r, :] = jnp.dot(
            probs, v_v[r].reshape(kv_here * span, hd), preferred_element_type=F32
        )
    for h in range(heads):
        att_all[me, :, h * hd : (h + 1) * hd] = att_h[h].astype(BF16)
    loads[3].wait()
    mine = pl.multiple_of(me * cols + s * part, 128)
    hid_all[me] = hid_v[:, pl.ds(mine, part)]

    pl.semaphore_wait(barrier, devs)

    def gather_start(buf, index, send_sem, recv_sem):
        block = buf.at[index(me)]
        out = []
        for k in FAR_ORDER:
            out.append(remote(block, block, send_sem.at[k], recv_sem.at[me], far_peer(k), s))
        out.append(remote(block, block, send_sem.at[far], recv_sem.at[me], beside, s))
        for copy in out:
            copy.start()
        return out

    def arrived(buf, index, recv_sem, p):
        block = buf.at[index(p)]
        remote(block, block, recv_sem.at[p], recv_sem.at[p], p, s).wait_recv()

    def relay(buf, index, send_sem, recv_sem, k):
        p = far_peer(k)
        arrived(buf, index, recv_sem, p)
        block = buf.at[index(p)]
        copy = remote(block, block, send_sem.at[far + k], recv_sem.at[p], beside, s)
        copy.start()
        return copy

    same = lambda p: p
    sends = gather_start(att_all, same, asend_sem, arecv_sem)
    for k in range(1, devs):
        p = peer(k)
        theirs = pl.multiple_of(p * cols + s * part, 128)
        copy = remote(
            hid_v.at[:, pl.ds(theirs, part)],
            hid_all.at[me],
            csend_sem.at[k],
            crecv_sem.at[me],
            p,
            s,
        )
        copy.start()
        sends.append(copy)
    loads[4].wait()
    low_copy = remote(lf_v.at[s], lf_v.at[s], psend_sem.at[1], precv_sem.at[1], me, mate)
    low_copy.start()
    sends.append(low_copy)
    for k in FAR_STEPS:
        sends.append(relay(att_all, same, asend_sem, arecv_sem, k))
    loads[5].wait()
    for k in range(1, devs):
        p = peer(k)
        remote(
            hid_all.at[p], hid_all.at[p], csend_sem.at[k], crecv_sem.at[p], p, s
        ).wait_recv()
    own_hidden = jnp.concatenate([hid_all[d].astype(F32) for d in range(devs)], axis=0)
    arrived(att_all, same, arecv_sem, beside)
    for k in FAR_STEPS:
        arrived(att_all, same, arecv_sem, far_beside(k))
    attended = jnp.concatenate(
        [att_all[d, :, :att_width].astype(F32) for d in range(devs)], axis=0
    ).astype(BF16)

    theirs = pl.multiple_of(mate * part, 128)
    pair_send[...] = jnp.dot(
        attended, op_v[:, pl.ds(theirs, part)], preferred_element_type=F32
    )
    pair_copy = remote(pair_send, pair_recv, psend_sem.at[0], precv_sem.at[0], me, mate)
    pair_copy.start()
    sends.append(pair_copy)
    ours = pl.multiple_of(s * part, 128)
    projected = own_hidden + jnp.dot(
        attended, op_v[:, pl.ds(ours, part)], preferred_element_type=F32
    )
    pair_copy.wait_recv()

    def block_of(p):
        return p * subs + s

    res_all[block_of(me)] = (projected + pair_recv[...]).astype(BF16)
    sends.extend(gather_start(res_all, block_of, gsend_sem, grecv_sem))

    def over(p, k):
        block = res_all.at[block_of(p)]
        copy = remote(block, block, fsend_sem.at[k], frecv_sem.at[p], me, mate)
        copy.start()
        return copy

    sends.append(over(me, 0))
    sq_v[...] = jnp.zeros_like(sq_v)
    low_v[...] = jnp.zeros_like(low_v)
    logit_v[...] = jnp.zeros_like(logit_v)
    acc[...] = jnp.zeros_like(acc)
    low_copy.wait_recv()

    def on_beside():
        arrived(res_all, block_of, grecv_sem, beside)
        over(beside, 1)

    def on_far(n):
        k = FAR_STEPS[n]
        relay(res_all, block_of, gsend_sem, grecv_sem, k)
        over(far_peer(k), 2 + n)

    def on_relayed(n):
        p = far_beside(FAR_STEPS[n])
        arrived(res_all, block_of, grecv_sem, p)
        over(p, far + 1 + n)

    events = {2: [on_beside]}
    for n in range(far - 1):
        events.setdefault(FAR_AT[n], []).append(functools.partial(on_far, n))
        events.setdefault(RELAYED_AT[n], []).append(functools.partial(on_relayed, n))

    def gate_step(i, carry):
        for when, actions in events.items():

            @pl.when(i == when)
            def _():
                for action in actions:
                    action()

        p = block_at(i // 2)
        odd = lax.rem(i, 2)

        @pl.when(odd == 0)
        def _():
            block = res_all.at[p * subs + mate]
            remote(block, block, frecv_sem.at[p], frecv_sem.at[p], me, mate).wait_recv()
            squares = sq_v[...]
            for b in range(subs):
                r = res_all[p * subs + b].astype(F32)
                at_cols = pl.ds(pl.multiple_of(p * cols + b * part, 128), part)
                x_v[:, b * part : (b + 1) * part] = (r * gain[:, at_cols]).astype(BF16)
                for c in range(part // 128):
                    v = r[:, c * 128 : (c + 1) * 128]
                    squares = squares + v * v
            sq_v[...] = squares
            per_half = half // cols
            at_rows = pl.ds(pl.multiple_of(lax.rem(p, per_half) * cols, cols), cols)
            x = x_v[...]
            low_v[...] += jnp.dot(x, lf_v[p // per_half, at_rows, :], preferred_element_type=F32)
            logit_v[...] += lax.dot_general(
                x,
                router[:, pl.ds(pl.multiple_of(p * cols, 128), cols)],
                (((1,), (1,)), ((), ())),
                preferred_element_type=F32,
            )

        slot = lax.rem(i, gate_slots)
        pltpu.make_async_copy(
            gate_w.at[pl.ds(0, cols)], ring_a.at[slot], a_sem.at[slot]
        ).wait()
        acc[odd] += jnp.dot(x_v[...], ring_a[slot], preferred_element_type=F32)

        @pl.when(i + gate_slots < gate_chunks)
        def _():
            start_a(i + gate_slots)

        return carry

    lax.fori_loop(0, gate_chunks, gate_step, 0)

    inverse = lax.rsqrt(jnp.sum(sq_v[...], axis=-1, keepdims=True) / width + EPSILON)
    low = (low_v[...] * inverse).astype(BF16)
    logits = logit_v[...] * inverse
    count = router.shape[0]
    label = lax.broadcasted_iota(jnp.int32, (all_rows, count), 1)
    named = jnp.concatenate(
        [att_all[d, :, att_width:].astype(F32) for d in range(devs)], axis=0
    ).astype(jnp.int32)
    e0 = named[:, 0:1]
    e1 = named[:, 1:2]
    a = jnp.sum(jnp.where(label == e0, logits, 0.0), axis=-1, keepdims=True)
    b = jnp.sum(jnp.where(label == e1, logits, 0.0), axis=-1, keepdims=True)
    lead = jax.nn.sigmoid(a - b)
    here = me // (devs // count)
    share = jnp.where(e0 == here, lead, 0.0) + jnp.where(e1 == here, 1.0 - lead, 0.0)

    loads[6].wait()
    loads[7].wait()
    for n in range(units // CHUNK):
        at_units = slice(n * CHUNK, (n + 1) * CHUNK)
        gate_sum = acc[0, :, at_units] * inverse + jnp.dot(
            low, gl_v[:, at_units], preferred_element_type=F32
        )
        up_sum = acc[1, :, at_units] * inverse + jnp.dot(
            low, ul_v[:, at_units], preferred_element_type=F32
        )
        inner[:, at_units] = (gate_sum / (1.0 + jnp.exp(-gate_sum)) * up_sum).astype(BF16)

    def down(i):
        slot = lax.rem(i, down_slots)
        pltpu.make_async_copy(
            down_w.at[:, pl.ds(0, CHUNK)], ring_b.at[slot], b_sem.at[slot]
        ).wait()
        product = jnp.dot(inner[...], ring_b[slot], preferred_element_type=F32) * share

        @pl.when(i + down_slots < down_chunks)
        def _():
            start_b(i + down_slots)

        return product

    def to_mate(i, c):
        dsend[c] = down(i).astype(BF16)
        remote(dsend.at[c], drecv.at[c], xsend_sem.at[c], xrecv_sem.at[c], me, mate).start()

    to_mate(0, 0)

    def down_step(c, carry):
        @pl.when(c < steps - 1)
        def _():
            to_mate(2 * c + 1, c + 1)

        kept = down(jnp.minimum(2 * c + 2, down_chunks - 1))
        remote(dsend.at[c], drecv.at[c], xsend_sem.at[c], xrecv_sem.at[c], me, mate).wait_recv()
        total = kept + drecv[c].astype(F32)
        for d in range(devs):
            rsend[c, d] = total[d * rows : (d + 1) * rows].astype(BF16)
        rrecv[c, me] = rsend[c, me]
        for k in range(1, devs):
            p = peer(k)
            remote(
                rsend.at[c, p], rrecv.at[c, me], rs_sem.at[c, k], rr_sem.at[c, me], p, s
            ).start()
        return carry

    lax.fori_loop(0, steps, down_step, 0)
    my_rows = pl.ds(pl.multiple_of(me * rows, rows), rows)
    for b in range(devs * subs):
        pair_recv[...] = res_all[b].astype(F32)
        residual[:, b * part : (b + 1) * part] = pair_recv[my_rows, :]

    def sum_step(c, carry):
        for k in range(1, devs):
            p = peer(k)
            remote(
                rsend.at[c, p], rrecv.at[c, p], rs_sem.at[c, k], rr_sem.at[c, p], p, s
            ).wait_recv()
        got = rrecv[c, 0].astype(F32)
        for d in range(1, devs):
            got = got + rrecv[c, d].astype(F32)
        at_cols = pl.ds(pl.multiple_of((2 * c + s) * CHUNK, CHUNK), CHUNK)
        mixture[:, at_cols] = got
        remote(
            mixture.at[:, at_cols],
            mixture.at[:, at_cols],
            msend_sem.at[c],
            mrecv_sem.at[c],
            me,
            mate,
        ).start()
        return carry

    lax.fori_loop(0, steps, sum_step, 0)

    for copy in sends:
        copy.wait_send()
    for k in FAR_STEPS:
        block = res_all.at[block_of(me)]
        remote(block, block, gsend_sem.at[far + k], grecv_sem.at[me], beside, s).wait_send()
    for k in range(1, devs):
        block = res_all.at[block_of(me)]
        remote(block, block, fsend_sem.at[k], frecv_sem.at[me], me, mate).wait_send()

    def last_step(c, carry):
        remote(dsend.at[c], drecv.at[c], xsend_sem.at[c], xrecv_sem.at[c], me, mate).wait_send()
        for k in range(1, devs):
            p = peer(k)
            remote(
                rsend.at[c, p], rrecv.at[c, me], rs_sem.at[c, k], rr_sem.at[c, me], p, s
            ).wait_send()
        at_cols = pl.ds(pl.multiple_of((2 * c + mate) * CHUNK, CHUNK), CHUNK)
        swap = remote(
            mixture.at[:, at_cols],
            mixture.at[:, at_cols],
            msend_sem.at[c],
            mrecv_sem.at[c],
            me,
            mate,
        )
        swap.wait()
        return carry

    lax.fori_loop(0, steps, last_step, 0)


def add_kernel(residual, mixture, layer_out, mixture_out):
    mixture_out[...] = mixture[...]
    layer_out[...] = (residual[...] + mixture[...]).astype(BF16)


def fits(mesh, shapes):
    devs, subs = mesh.shape["dev"], mesh.shape["sub"]
    hidden, query, keys, out_proj, router, gate_w, low_factor = shapes
    width = hidden[1]
    units = gate_w[1]
    cols = out_proj[1]
    return (
        subs == 2
        and devs == 4 * NEAR
        and devs * hidden[0] <= 128
        and hidden[0] == 8
        and query[2] == 128
        and cols % (128 * subs) == 0
        and cols * devs == width
        and low_factor[0] % cols == 0
        and units % CHUNK == 0
        and width % (2 * CHUNK) == 0
        and devs % router[1] == 0
        and (GATE_SLOTS * cols + DOWN_SLOTS * CHUNK) * units * 2 <= 48 * 10**6
    )


def body(mesh, *args):
    (
        hidden,
        query,
        keys,
        values,
        lengths,
        out_proj,
        gain,
        router,
        low_factor,
        gate_w,
        up_w,
        down_w,
        gate_low,
        up_low,
        experts,
    ) = args
    shapes = [x.shape for x in (hidden, query, keys, out_proj, router, gate_w, low_factor)]
    if not fits(mesh, shapes):
        return plain_body(*args)
    devs, subs = mesh.shape["dev"], mesh.shape["sub"]
    rows, width = hidden.shape
    all_rows = devs * rows
    heads, hd = query.shape[1:]
    cols = out_proj.shape[1]
    part = cols // subs
    units = gate_w.shape[1]
    half, rank = low_factor.shape
    steps = width // (2 * CHUNK)
    gate_slots = min(2 * devs, GATE_SLOTS)
    down_slots = min(2 * steps, DOWN_SLOTS)
    anywhere = pl.BlockSpec(memory_space=pl.ANY)
    vmem = pl.BlockSpec(memory_space=pltpu.VMEM)
    smem = pl.BlockSpec(memory_space=pltpu.SMEM)
    dma = pltpu.SemaphoreType.DMA
    scratch = [
        pltpu.VMEM((gate_slots, cols, units), BF16),
        pltpu.VMEM((down_slots, units, CHUNK), BF16),
        pltpu.VMEM(hidden.shape, BF16),
        pltpu.VMEM(query.shape, BF16),
        pltpu.VMEM(keys.shape, BF16),
        pltpu.VMEM(values.shape, BF16),
        pltpu.VMEM(out_proj.shape, BF16),
        pltpu.VMEM((subs, half, rank), BF16),
        pltpu.VMEM(gate_low.shape, BF16),
        pltpu.VMEM(up_low.shape, BF16),
        pltpu.VMEM((heads, rows, hd), F32),
        pltpu.VMEM((devs, rows, heads * hd + 128), BF16),
        pltpu.VMEM((devs, rows, part), BF16),
        pltpu.VMEM((all_rows, part), F32),
        pltpu.VMEM((all_rows, part), F32),
        pltpu.VMEM((devs * subs, all_rows, part), BF16),
        pltpu.VMEM((all_rows, cols), BF16),
        pltpu.VMEM((all_rows, 128), F32),
        pltpu.VMEM((all_rows, rank), F32),
        pltpu.VMEM((all_rows, router.shape[1]), F32),
        pltpu.VMEM((2, all_rows, units), F32),
        pltpu.VMEM((all_rows, units), BF16),
        pltpu.VMEM((steps, all_rows, CHUNK), BF16),
        pltpu.VMEM((steps, all_rows, CHUNK), BF16),
        pltpu.VMEM((steps, devs, rows, CHUNK), BF16),
        pltpu.VMEM((steps, devs, rows, CHUNK), BF16),
        dma((8,)),
        dma((gate_slots,)),
        dma((down_slots,)),
    ]
    scratch += [dma((devs,)) for _ in range(8)]
    scratch += [dma((2,)), dma((2,)), dma((steps,)), dma((steps,))]
    scratch += [dma((steps, devs)), dma((steps, devs))]
    scratch += [dma((steps,)), dma((steps,))]
    residual, mixture = pl.pallas_call(
        functools.partial(layer_kernel, devs, subs, gate_slots, down_slots),
        out_shape=(
            jax.ShapeDtypeStruct((rows, width), F32),
            jax.ShapeDtypeStruct((rows, width), F32),
        ),
        in_specs=[anywhere] * 4
        + [smem, anywhere, vmem, vmem]
        + [anywhere] * 6
        + [smem],
        out_specs=(vmem, vmem),
        scratch_shapes=scratch,
        compiler_params=pltpu.CompilerParams(
            collective_id=0, has_side_effects=True, vmem_limit_bytes=VMEM_BYTES
        ),
    )(
        hidden,
        query,
        keys,
        values,
        lengths,
        out_proj,
        gain.reshape(1, width),
        router.T,
        low_factor,
        gate_w,
        up_w,
        down_w,
        gate_low,
        up_low,
        experts.T,
    )
    return pl.pallas_call(
        add_kernel,
        out_shape=(
            jax.ShapeDtypeStruct((rows, width), BF16),
            jax.ShapeDtypeStruct((rows, width), F32),
        ),
        in_specs=[vmem, vmem],
        out_specs=(vmem, vmem),
    )(residual, mixture)


def solution(mesh):
    placed = (
        P(("groups", "dev"), None),
        P(("groups", "dev"), "sub", None),
        P(("groups", "dev"), "sub", None, None),
        P(("groups", "dev"), "sub", None, None),
        P(("groups", "dev")),
        P("sub", "dev"),
        P(),
        P(),
        P("sub", None),
        P(None, ("dev", "sub")),
        P(None, ("dev", "sub")),
        P(("dev", "sub"), None),
        P(None, ("dev", "sub")),
        P(None, ("dev", "sub")),
        P(("groups", "dev"), None),
    )
    return jax.shard_map(
        functools.partial(body, mesh),
        mesh=mesh,
        in_specs=placed,
        out_specs=(P(("groups", "dev"), None), P(("groups", "dev"), None)),
        check_vma=False,
    )
```

```python
import functools

import jax
import jax.numpy as jnp
from jax import lax
from jax.experimental import pallas as pl
from jax.experimental.pallas import tpu as pltpu
from jax.sharding import PartitionSpec as P

CAP = 6


EPSILON = 1e-05


def expert_shard(row_block, low_rank, gate_weight, up_weight, down_weight, gate_low, up_low):
    gate_sum = jnp.dot(row_block, gate_weight, preferred_element_type=jnp.float32) + jnp.dot(
        low_rank, gate_low, preferred_element_type=jnp.float32
    )
    up_sum = jnp.dot(row_block, up_weight, preferred_element_type=jnp.float32) + jnp.dot(
        low_rank, up_low, preferred_element_type=jnp.float32
    )
    inner_act = (jax.nn.silu(gate_sum) * up_sum).astype(jnp.bfloat16)
    return jnp.dot(inner_act, down_weight, preferred_element_type=jnp.float32)


def route_gates(normed, router, experts):
    logits = jnp.dot(normed, router, preferred_element_type=jnp.float32)
    labels = lax.broadcasted_iota(jnp.int32, (1, 1, router.shape[1]), 2)
    picked = (experts[:, :, None] == labels).astype(jnp.float32)
    chosen = jnp.sum(logits[:, None, :] * picked, axis=-1)
    leading = jax.nn.sigmoid(chosen[:, 0] - chosen[:, 1])
    return jnp.stack([leading, 1.0 - leading], axis=-1)


def plain_body(
    hidden,
    query,
    cache_keys,
    cache_values,
    lengths,
    out_proj,
    norm_gain,
    router,
    low_factor,
    gate_weight,
    up_weight,
    down_weight,
    gate_low,
    up_low,
    experts,
):
    requests = hidden.shape[0]
    model_width = hidden.shape[1]
    heads_here = query.shape[1]
    kv_here = cache_keys.shape[1]
    span_len = cache_keys.shape[2]
    head_size = query.shape[2]
    grouped = query.reshape(requests, kv_here, heads_here // kv_here, head_size)
    scores = jnp.einsum(
        "rkgd,rkld->rkgl", grouped, cache_keys, preferred_element_type=jnp.float32
    ) * head_size ** (-0.5)
    visible = lax.broadcasted_iota(jnp.int32, (requests, span_len), 1) < lengths[:, None]
    scores = jnp.where(visible[:, None, None, :], scores, -1e30)
    attn_probs = jax.nn.softmax(scores, axis=-1).astype(jnp.bfloat16)
    attended = jnp.einsum(
        "rkgl,rkld->rkgd", attn_probs, cache_values, preferred_element_type=jnp.float32
    )
    attended = attended.astype(jnp.bfloat16).reshape(requests, heads_here * head_size)
    columns = jnp.dot(
        lax.all_gather(attended, "dev", axis=0, tiled=True),
        out_proj,
        preferred_element_type=jnp.float32,
    )
    partial_proj = lax.all_to_all(columns, "dev", split_axis=0, concat_axis=1, tiled=True)
    residual = hidden.astype(jnp.float32) + lax.psum(partial_proj, "sub")
    inverse = lax.rsqrt(jnp.mean(residual * residual, axis=-1, keepdims=True) + EPSILON)
    normed = (residual * inverse * norm_gain).astype(jnp.bfloat16)
    half_width = low_factor.shape[0]
    normed_half = lax.dynamic_slice_in_dim(
        normed, lax.axis_index("sub") * half_width, half_width, 1
    )
    low_partial = jnp.dot(normed_half, low_factor, preferred_element_type=jnp.float32)
    low_rank = lax.psum(low_partial, "sub").astype(jnp.bfloat16)
    rank_width = low_rank.shape[1]
    expert_count = router.shape[1]
    holders = lax.axis_size("dev") // expert_count
    gate_pair = route_gates(normed, router, experts)
    flat_ids = experts.reshape(-1)
    entries = flat_ids.shape[0]
    same_expert = flat_ids[:, None] == flat_ids[None, :]
    earlier = lax.broadcasted_iota(jnp.int32, (entries, entries), 0) > lax.broadcasted_iota(
        jnp.int32, (entries, entries), 1
    )
    slot_index = jnp.sum((same_expert & earlier).astype(jnp.int32), axis=1).reshape(requests, 2)
    target = experts * CAP + slot_index
    placement = (
        target[:, :, None] == lax.broadcasted_iota(jnp.int32, (1, 1, expert_count * CAP), 2)
    ).astype(jnp.float32)
    chosen = jnp.sum(placement, axis=1).astype(jnp.bfloat16)
    packed_rows = jnp.einsum(
        "rs,rd->sd", chosen, normed, preferred_element_type=jnp.float32
    ).astype(jnp.bfloat16)
    packed_low = jnp.einsum(
        "rs,rd->sd", chosen, low_rank, preferred_element_type=jnp.float32
    ).astype(jnp.bfloat16)
    send_rows = jnp.repeat(packed_rows.reshape(expert_count, CAP, model_width), holders, axis=0)
    send_low = jnp.repeat(packed_low.reshape(expert_count, CAP, rank_width), holders, axis=0)
    got_rows = lax.all_to_all(send_rows, "dev", split_axis=0, concat_axis=0, tiled=True)
    got_low = lax.all_to_all(send_low, "dev", split_axis=0, concat_axis=0, tiled=True)
    sources = got_rows.shape[0]
    slot_count = got_rows.shape[1]
    result = expert_shard(
        got_rows.reshape(sources * slot_count, model_width),
        got_low.reshape(sources * slot_count, rank_width),
        gate_weight,
        up_weight,
        down_weight,
        gate_low,
        up_low,
    )
    partials = result.reshape(sources, slot_count, model_width)
    returned = lax.all_to_all(
        partials.astype(jnp.bfloat16), "dev", split_axis=0, concat_axis=0, tiled=True
    ).astype(partials.dtype)
    per_slot = jnp.sum(returned.reshape(expert_count, holders, CAP, model_width), axis=1).reshape(
        expert_count * CAP, model_width
    )
    weighted = jnp.sum(placement * gate_pair[:, :, None], axis=1)
    mixture_part = jnp.dot(weighted, per_slot, precision=lax.Precision.HIGHEST)
    mixture = lax.psum(mixture_part.astype(jnp.bfloat16), "sub").astype(jnp.float32)
    return ((residual + mixture).astype(jnp.bfloat16), mixture)


CHUNK = 512
NEAR = 2
FAR_ORDER = (2, 3, 1)
FAR_STEPS = (1, 3, 2)
GATE_SLOTS = 15
GATE_COLS = 512
SPLIT = 3
VMEM_BYTES = 66 * 10**6
F32 = jnp.float32
BF16 = jnp.bfloat16


def layer_kernel(
    devs,
    subs,
    gate_slots,
    hidden,
    query,
    keys,
    values,
    lengths,
    out_proj,
    gain_hbm,
    router_hbm,
    low_factor,
    gate_w,
    up_w,
    down_w,
    gate_low,
    up_low,
    experts,
    residual,
    mixture,
    ring,
    gain,
    router,
    hid_v,
    q_v,
    k_v,
    v_v,
    op_v,
    lf_v,
    gl_v,
    ul_v,
    att_h,
    att_all,
    hid_all,
    pair_send,
    pair_recv,
    res_all,
    x_v,
    sq_v,
    low_v,
    logit_v,
    acc,
    inner,
    dsend,
    drecv,
    rsend,
    rrecv,
    load_sem,
    a_sem,
    b_sem,
    csend_sem,
    crecv_sem,
    asend_sem,
    arecv_sem,
    gsend_sem,
    grecv_sem,
    fsend_sem,
    frecv_sem,
    psend_sem,
    precv_sem,
    xsend_sem,
    xrecv_sem,
    rs_sem,
    rr_sem,
    msend_sem,
    mrecv_sem,
):
    me = lax.axis_index("dev")
    s = lax.axis_index("sub")
    mate = 1 - s
    rows, width = hidden.shape
    all_rows = devs * rows
    heads = query.shape[1]
    kv_here, span, hd = keys.shape[1:]
    per_kv = heads // kv_here
    att_width = heads * hd
    cols = out_proj.shape[1]
    part = cols // subs
    units = gate_w.shape[1]
    half = low_factor.shape[0]
    steps = width // (2 * CHUNK)
    gate_chunks = 2 * devs

    far = devs // NEAR
    z = me // NEAR
    y = lax.rem(me, NEAR)
    beside = me + 1 - 2 * y

    def far_z(k):
        if k == 1:
            return z + 1 - 2 * lax.rem(z, 2)
        if k == 2:
            return lax.rem(z + 2, far)
        return far - 1 - z

    def far_peer(k):
        return far_z(k) * NEAR + y

    def far_beside(k):
        return far_z(k) * NEAR + 1 - y

    def peer(k):
        return lax.rem(me + k, devs)

    def remote(src, dst, send_sem, recv_sem, d, sub):
        return pltpu.make_async_remote_copy(
            src_ref=src,
            dst_ref=dst,
            send_sem=send_sem,
            recv_sem=recv_sem,
            device_id={"dev": d, "sub": sub},
            device_id_type=pl.DeviceIdType.MESH,
        )

    barrier = pltpu.get_barrier_semaphore()
    for k in range(1, devs):
        pl.semaphore_signal(
            barrier, inc=1, device_id={"dev": peer(k), "sub": s}, device_id_type=pl.DeviceIdType.MESH
        )
    pl.semaphore_signal(
        barrier, inc=1, device_id={"dev": me, "sub": mate}, device_id_type=pl.DeviceIdType.MESH
    )

    loads = [
        pltpu.make_async_copy(src, dst, load_sem.at[n])
        for n, (src, dst) in enumerate(
            [
                (query, q_v),
                (keys, k_v),
                (values, v_v),
                (hidden, hid_v),
                (low_factor, lf_v.at[s]),
                (out_proj, op_v),
                (gate_low, gl_v),
                (up_low, ul_v),
                (gain_hbm, gain),
                (router_hbm, router),
            ]
        )
    ]
    for load in loads:
        load.start()

    def block_at(k):
        kz = jnp.where(k < 2, 0, lax.rem(k - 2, far - 1) + 1)
        beside_too = jnp.where(k < 2, k, jnp.where(k < far + 1, 0, 1))
        zz = z
        for n, f in enumerate(FAR_STEPS):
            zz = jnp.where(kz == n + 1, far_z(f), zz)
        return zz * NEAR + lax.rem(y + beside_too, NEAR)

    group_cols = units
    groups = width // group_cols
    sub_rows = cols // SPLIT
    per_group = units // sub_rows
    down_base = gate_chunks * SPLIT - gate_slots * SPLIT

    def start_a(i):
        slot = lax.rem(i, gate_slots)
        at_rows = pl.ds(pl.multiple_of(block_at(i // 2) * cols, cols), cols)
        to_rows = pl.ds(pl.multiple_of(slot * cols, cols), cols)

        @pl.when(lax.rem(i, 2) == 0)
        def _():
            pltpu.make_async_copy(gate_w.at[at_rows], ring.at[to_rows], a_sem.at[slot]).start()

        @pl.when(lax.rem(i, 2) == 1)
        def _():
            pltpu.make_async_copy(up_w.at[at_rows], ring.at[to_rows], a_sem.at[slot]).start()

    def start_down(t):
        g = t // per_group
        at_rows = pl.ds(pl.multiple_of(lax.rem(t, per_group) * sub_rows, sub_rows), sub_rows)
        at_cols = pl.ds(pl.multiple_of(g * group_cols, 128), group_cols)
        to_rows = pl.ds(pl.multiple_of((down_base + t) * sub_rows, sub_rows), sub_rows)
        pltpu.make_async_copy(down_w.at[at_rows, at_cols], ring.at[to_rows], b_sem.at[g]).start()

    def refill(i):
        @pl.when(i + gate_slots < gate_chunks)
        def _():
            start_a(i + gate_slots)

        for t in range(SPLIT):
            at = (i + gate_slots - gate_chunks) * SPLIT + t

            @pl.when((at >= 0) & (at < groups * per_group))
            def _():
                start_down(at)

    def first_load(i, carry):
        start_a(i)
        return carry

    lax.fori_loop(0, gate_slots, first_load, 0)

    lane = lax.broadcasted_iota(jnp.int32, (rows, 128), 1)
    row = lax.broadcasted_iota(jnp.int32, (rows, 128), 0)
    named = jnp.zeros((rows, 128), jnp.int32)
    for r in range(rows):
        named = jnp.where(row == r, jnp.where(lane == 0, experts[0, r], experts[1, r]), named)
    att_all[me, :, att_width:] = named.astype(F32).astype(BF16)

    for load in loads[:3]:
        load.wait()
    at = lax.broadcasted_iota(jnp.int32, (heads, kv_here * span), 1)
    head = lax.broadcasted_iota(jnp.int32, (heads, kv_here * span), 0)
    place = jnp.where((at // span) == (head // per_kv), at % span, span)
    each = range(rows)
    scores = [
        lax.dot_general(
            q_v[r],
            k_v[r].reshape(kv_here * span, hd),
            (((1,), (1,)), ((), ())),
            preferred_element_type=F32,
        )
        for r in each
    ]
    scores = [jnp.where(place < lengths[r], scores[r] * hd ** (-0.5), -1e30) for r in each]
    top = [jnp.max(scores[r], axis=-1, keepdims=True) for r in each]
    grown = [jnp.exp(scores[r] - top[r]) for r in each]
    scale = [1.0 / jnp.sum(grown[r], axis=-1, keepdims=True) for r in each]
    probs = [(grown[r] * scale[r]).astype(BF16) for r in each]
    mixed = [
        jnp.dot(probs[r], v_v[r].reshape(kv_here * span, hd), preferred_element_type=F32)
        for r in each
    ]
    for r in each:
        att_h[:, r, :] = mixed[r]
    for h in range(heads):
        att_all[me, :, h * hd : (h + 1) * hd] = att_h[h].astype(BF16)
    loads[3].wait()
    mine = pl.multiple_of(me * cols + s * part, 128)
    hid_all[me] = hid_v[:, pl.ds(mine, part)]

    pl.semaphore_wait(barrier, devs)

    def gather_start(buf, index, send_sem, recv_sem):
        block = buf.at[index(me)]
        out = []
        for k in FAR_ORDER:
            out.append(remote(block, block, send_sem.at[k], recv_sem.at[me], far_peer(k), s))
        out.append(remote(block, block, send_sem.at[far], recv_sem.at[me], beside, s))
        for copy in out:
            copy.start()
        return out

    def arrived(buf, index, recv_sem, p):
        block = buf.at[index(p)]
        remote(block, block, recv_sem.at[p], recv_sem.at[p], p, s).wait_recv()

    def relay(buf, index, send_sem, recv_sem, k):
        p = far_peer(k)
        arrived(buf, index, recv_sem, p)
        block = buf.at[index(p)]
        copy = remote(block, block, send_sem.at[far + k], recv_sem.at[p], beside, s)
        copy.start()
        return copy

    same = lambda p: p
    sends = gather_start(att_all, same, asend_sem, arecv_sem)
    for k in range(1, devs):
        p = peer(k)
        theirs = pl.multiple_of(p * cols + s * part, 128)
        copy = remote(
            hid_v.at[:, pl.ds(theirs, part)],
            hid_all.at[me],
            csend_sem.at[k],
            crecv_sem.at[me],
            p,
            s,
        )
        copy.start()
        sends.append(copy)
    loads[4].wait()
    low_copy = remote(lf_v.at[s], lf_v.at[s], psend_sem.at[1], precv_sem.at[1], me, mate)
    low_copy.start()
    sends.append(low_copy)
    for k in FAR_STEPS:
        sends.append(relay(att_all, same, asend_sem, arecv_sem, k))
    loads[5].wait()
    for k in range(1, devs):
        p = peer(k)
        remote(
            hid_all.at[p], hid_all.at[p], csend_sem.at[k], crecv_sem.at[p], p, s
        ).wait_recv()
    own_hidden = jnp.concatenate([hid_all[d].astype(F32) for d in range(devs)], axis=0)
    arrived(att_all, same, arecv_sem, beside)
    for k in FAR_STEPS:
        arrived(att_all, same, arecv_sem, far_beside(k))
    attended = jnp.concatenate(
        [att_all[d, :, :att_width].astype(F32) for d in range(devs)], axis=0
    ).astype(BF16)

    theirs = pl.multiple_of(mate * part, 128)
    pair_send[...] = jnp.dot(
        attended, op_v[:, pl.ds(theirs, part)], preferred_element_type=F32
    )
    pair_copy = remote(pair_send, pair_recv, psend_sem.at[0], precv_sem.at[0], me, mate)
    pair_copy.start()
    sends.append(pair_copy)
    ours = pl.multiple_of(s * part, 128)
    projected = own_hidden + jnp.dot(
        attended, op_v[:, pl.ds(ours, part)], preferred_element_type=F32
    )
    pair_copy.wait_recv()

    def block_of(p):
        return p * subs + s

    res_all[block_of(me)] = (projected + pair_recv[...]).astype(BF16)
    own_block = res_all.at[block_of(me)]
    for k in range(1, devs):
        copy = remote(
            own_block, own_block, gsend_sem.at[k], grecv_sem.at[me], block_at(jnp.int32(k)), s
        )
        copy.start()
        sends.append(copy)

    def over(p, k):
        block = res_all.at[block_of(p)]
        copy = remote(block, block, fsend_sem.at[k], frecv_sem.at[p], me, mate)
        copy.start()
        return copy

    sends.append(over(me, 0))
    sq_v[...] = jnp.zeros_like(sq_v)
    low_v[...] = jnp.zeros_like(low_v)
    logit_v[...] = jnp.zeros_like(logit_v)
    acc[...] = jnp.zeros_like(acc)
    low_copy.wait_recv()

    def await_a(i):
        slot = lax.rem(i, gate_slots)
        at_rows = pl.ds(pl.multiple_of(slot * cols, cols), cols)
        pltpu.make_async_copy(
            gate_w.at[pl.ds(0, cols)], ring.at[at_rows], a_sem.at[slot]
        ).wait()
        return at_rows

    def arrive_next(k):
        @pl.when(k < devs - 1)
        def _():
            p = block_at(k + 1)
            arrived(res_all, block_of, grecv_sem, p)
            over(p, k + 1)

    per_half = half // cols
    loads[6].wait()
    loads[7].wait()
    loads[8].wait()
    loads[9].wait()

    def gate_step(k, carry):
        p = block_at(k)
        block = res_all.at[p * subs + mate]
        remote(block, block, frecv_sem.at[p], frecv_sem.at[p], me, mate).wait_recv()
        weights = await_a(2 * k)
        squares = sq_v[...]
        pieces = []
        for b in range(subs):
            r = res_all[p * subs + b].astype(F32)
            at_cols = pl.ds(pl.multiple_of(p * cols + b * part, 128), part)
            pieces.append((r * gain[:, at_cols]).astype(BF16))
            for c in range(part // 128):
                v = r[:, c * 128 : (c + 1) * 128]
                squares = squares + v * v
        sq_v[...] = squares
        x = jnp.concatenate(pieces, axis=1)
        x_v[...] = x
        at_rows = pl.ds(pl.multiple_of(lax.rem(p, per_half) * cols, cols), cols)
        at_cols = pl.ds(pl.multiple_of(p * cols, 128), cols)
        for n in range(0, units, GATE_COLS):
            acc[0, :, n : n + GATE_COLS] += jnp.dot(
                x, ring[weights, n : n + GATE_COLS], preferred_element_type=F32
            )
        low_v[...] += jnp.dot(x, lf_v[p // per_half, at_rows, :], preferred_element_type=F32)
        logit_v[...] += lax.dot_general(
            x, router[:, at_cols], (((1,), (1,)), ((), ())), preferred_element_type=F32
        )
        refill(2 * k)
        arrive_next(k)
        weights = await_a(2 * k + 1)
        x = x_v[...]
        for n in range(0, units, GATE_COLS):
            acc[1, :, n : n + GATE_COLS] += jnp.dot(
                x, ring[weights, n : n + GATE_COLS], preferred_element_type=F32
            )
        refill(2 * k + 1)
        return carry

    lax.fori_loop(0, devs, gate_step, 0)

    inverse = lax.rsqrt(jnp.sum(sq_v[...], axis=-1, keepdims=True) / width + EPSILON)
    low = (low_v[...] * inverse).astype(BF16)
    logits = logit_v[...] * inverse
    count = router.shape[0]
    label = lax.broadcasted_iota(jnp.int32, (all_rows, count), 1)
    named = jnp.concatenate(
        [att_all[d, :, att_width:].astype(F32) for d in range(devs)], axis=0
    ).astype(jnp.int32)
    e0 = named[:, 0:1]
    e1 = named[:, 1:2]
    a = jnp.sum(jnp.where(label == e0, logits, 0.0), axis=-1, keepdims=True)
    b = jnp.sum(jnp.where(label == e1, logits, 0.0), axis=-1, keepdims=True)
    lead = jax.nn.sigmoid(a - b)
    here = me // (devs // count)
    share = jnp.where(e0 == here, lead, 0.0) + jnp.where(e1 == here, 1.0 - lead, 0.0)

    for n in range(units // CHUNK):
        at_units = slice(n * CHUNK, (n + 1) * CHUNK)
        gate_sum = acc[0, :, at_units] * inverse + jnp.dot(
            low, gl_v[:, at_units], preferred_element_type=F32
        )
        up_sum = acc[1, :, at_units] * inverse + jnp.dot(
            low, ul_v[:, at_units], preferred_element_type=F32
        )
        inner[:, at_units] = (gate_sum / (1.0 + jnp.exp(-gate_sum)) * up_sum).astype(BF16)

    pairs_in = group_cols // (2 * CHUNK)

    def down(c, whose):
        at_rows = pl.ds(
            pl.multiple_of((down_base + c // pairs_in * per_group) * sub_rows, sub_rows), units
        )
        at_cols = pl.ds(
            pl.multiple_of((2 * lax.rem(c, pairs_in) + whose) * CHUNK, CHUNK), CHUNK
        )
        return jnp.dot(inner[...], ring[at_rows, at_cols], preferred_element_type=F32) * share

    def to_mate(c):
        @pl.when(lax.rem(c, pairs_in) == 0)
        def _():
            g = c // pairs_in
            pltpu.make_async_copy(
                down_w.at[:, pl.ds(0, group_cols)], ring.at[pl.ds(0, units)], b_sem.at[g]
            ).wait()

        dsend[c] = down(c, mate).astype(BF16)
        remote(dsend.at[c], drecv.at[c], xsend_sem.at[c], xrecv_sem.at[c], me, mate).start()

    to_mate(jnp.int32(0))

    def down_step(c, carry):
        @pl.when(c < steps - 1)
        def _():
            to_mate(c + 1)

        kept = down(c, s)
        remote(dsend.at[c], drecv.at[c], xsend_sem.at[c], xrecv_sem.at[c], me, mate).wait_recv()
        total = kept + drecv[c].astype(F32)
        for d in range(devs):
            rsend[c, d] = total[d * rows : (d + 1) * rows].astype(BF16)
        rrecv[c, me] = rsend[c, me]
        for k in range(1, devs):
            p = peer(k)
            remote(
                rsend.at[c, p], rrecv.at[c, me], rs_sem.at[c, k], rr_sem.at[c, me], p, s
            ).start()
        return carry

    lax.fori_loop(0, steps, down_step, 0)
    my_rows = pl.ds(pl.multiple_of(me * rows, rows), rows)
    for b in range(devs * subs):
        pair_recv[...] = res_all[b].astype(F32)
        residual[:, b * part : (b + 1) * part] = pair_recv[my_rows, :]

    def sum_step(c, carry):
        for k in range(1, devs):
            p = peer(k)
            remote(
                rsend.at[c, p], rrecv.at[c, p], rs_sem.at[c, k], rr_sem.at[c, p], p, s
            ).wait_recv()
        got = rrecv[c, 0].astype(F32)
        for d in range(1, devs):
            got = got + rrecv[c, d].astype(F32)
        at_cols = pl.ds(pl.multiple_of((2 * c + s) * CHUNK, CHUNK), CHUNK)
        mixture[:, at_cols] = got
        remote(
            mixture.at[:, at_cols],
            mixture.at[:, at_cols],
            msend_sem.at[c],
            mrecv_sem.at[c],
            me,
            mate,
        ).start()
        return carry

    lax.fori_loop(0, steps, sum_step, 0)

    for copy in sends:
        copy.wait_send()
    for k in range(1, devs):
        block = res_all.at[block_of(me)]
        remote(block, block, fsend_sem.at[k], frecv_sem.at[me], me, mate).wait_send()

    def last_step(c, carry):
        remote(dsend.at[c], drecv.at[c], xsend_sem.at[c], xrecv_sem.at[c], me, mate).wait_send()
        for k in range(1, devs):
            p = peer(k)
            remote(
                rsend.at[c, p], rrecv.at[c, me], rs_sem.at[c, k], rr_sem.at[c, me], p, s
            ).wait_send()
        at_cols = pl.ds(pl.multiple_of((2 * c + mate) * CHUNK, CHUNK), CHUNK)
        swap = remote(
            mixture.at[:, at_cols],
            mixture.at[:, at_cols],
            msend_sem.at[c],
            mrecv_sem.at[c],
            me,
            mate,
        )
        swap.wait()
        return carry

    lax.fori_loop(0, steps, last_step, 0)


def add_kernel(residual, mixture, layer_out, mixture_out):
    mixture_out[...] = mixture[...]
    layer_out[...] = (residual[...] + mixture[...]).astype(BF16)


def fits(mesh, shapes):
    devs, subs = mesh.shape["dev"], mesh.shape["sub"]
    hidden, query, keys, out_proj, router, gate_w, low_factor = shapes
    width = hidden[1]
    units = gate_w[1]
    cols = out_proj[1]
    return (
        subs == 2
        and devs == 4 * NEAR
        and devs * hidden[0] <= 128
        and hidden[0] == 8
        and query[2] == 128
        and cols % (128 * subs) == 0
        and cols * devs == width
        and low_factor[0] % cols == 0
        and units % CHUNK == 0
        and width % (2 * CHUNK) == 0
        and devs % router[1] == 0
        and cols % (16 * SPLIT) == 0
        and units % (cols // SPLIT) == 0
        and width % units == 0
        and units % (2 * CHUNK) == 0
        and GATE_SLOTS * cols * units * 2 <= 48 * 10**6
        and GATE_SLOTS < 2 * devs
        and width // units * (units // (cols // SPLIT)) <= (2 * GATE_SLOTS - 2 * devs) * SPLIT
    )


def body(mesh, *args):
    (
        hidden,
        query,
        keys,
        values,
        lengths,
        out_proj,
        gain,
        router,
        low_factor,
        gate_w,
        up_w,
        down_w,
        gate_low,
        up_low,
        experts,
    ) = args
    shapes = [x.shape for x in (hidden, query, keys, out_proj, router, gate_w, low_factor)]
    if not fits(mesh, shapes):
        return plain_body(*args)
    devs, subs = mesh.shape["dev"], mesh.shape["sub"]
    rows, width = hidden.shape
    all_rows = devs * rows
    heads, hd = query.shape[1:]
    cols = out_proj.shape[1]
    part = cols // subs
    units = gate_w.shape[1]
    half, rank = low_factor.shape
    steps = width // (2 * CHUNK)
    anywhere = pl.BlockSpec(memory_space=pl.ANY)
    vmem = pl.BlockSpec(memory_space=pltpu.VMEM)
    smem = pl.BlockSpec(memory_space=pltpu.SMEM)
    dma = pltpu.SemaphoreType.DMA
    scratch = [
        pltpu.VMEM((GATE_SLOTS * cols, units), BF16),
        pltpu.VMEM((1, width), F32),
        pltpu.VMEM((router.shape[1], width), BF16),
        pltpu.VMEM(hidden.shape, BF16),
        pltpu.VMEM(query.shape, BF16),
        pltpu.VMEM(keys.shape, BF16),
        pltpu.VMEM(values.shape, BF16),
        pltpu.VMEM(out_proj.shape, BF16),
        pltpu.VMEM((subs, half, rank), BF16),
        pltpu.VMEM(gate_low.shape, BF16),
        pltpu.VMEM(up_low.shape, BF16),
        pltpu.VMEM((heads, rows, hd), F32),
        pltpu.VMEM((devs, rows, heads * hd + 128), BF16),
        pltpu.VMEM((devs, rows, part), BF16),
        pltpu.VMEM((all_rows, part), F32),
        pltpu.VMEM((all_rows, part), F32),
        pltpu.VMEM((devs * subs, all_rows, part), BF16),
        pltpu.VMEM((all_rows, cols), BF16),
        pltpu.VMEM((all_rows, 128), F32),
        pltpu.VMEM((all_rows, rank), F32),
        pltpu.VMEM((all_rows, router.shape[1]), F32),
        pltpu.VMEM((2, all_rows, units), F32),
        pltpu.VMEM((all_rows, units), BF16),
        pltpu.VMEM((steps, all_rows, CHUNK), BF16),
        pltpu.VMEM((steps, all_rows, CHUNK), BF16),
        pltpu.VMEM((steps, devs, rows, CHUNK), BF16),
        pltpu.VMEM((steps, devs, rows, CHUNK), BF16),
        dma((10,)),
        dma((GATE_SLOTS,)),
        dma((width // units,)),
    ]
    scratch += [dma((devs,)) for _ in range(8)]
    scratch += [dma((2,)), dma((2,)), dma((steps,)), dma((steps,))]
    scratch += [dma((steps, devs)), dma((steps, devs))]
    scratch += [dma((steps,)), dma((steps,))]
    residual, mixture = pl.pallas_call(
        functools.partial(layer_kernel, devs, subs, GATE_SLOTS),
        out_shape=(
            jax.ShapeDtypeStruct((rows, width), F32),
            jax.ShapeDtypeStruct((rows, width), F32),
        ),
        in_specs=[anywhere] * 4
        + [smem]
        + [anywhere] * 9
        + [smem],
        out_specs=(vmem, vmem),
        scratch_shapes=scratch,
        compiler_params=pltpu.CompilerParams(
            collective_id=0, has_side_effects=True, vmem_limit_bytes=VMEM_BYTES
        ),
    )(
        hidden,
        query,
        keys,
        values,
        lengths,
        out_proj,
        gain.reshape(1, width),
        router.T,
        low_factor,
        gate_w,
        up_w,
        down_w,
        gate_low,
        up_low,
        experts.T,
    )
    return pl.pallas_call(
        add_kernel,
        out_shape=(
            jax.ShapeDtypeStruct((rows, width), BF16),
            jax.ShapeDtypeStruct((rows, width), F32),
        ),
        in_specs=[vmem, vmem],
        out_specs=(vmem, vmem),
    )(residual, mixture)


def solution(mesh):
    placed = (
        P(("groups", "dev"), None),
        P(("groups", "dev"), "sub", None),
        P(("groups", "dev"), "sub", None, None),
        P(("groups", "dev"), "sub", None, None),
        P(("groups", "dev")),
        P("sub", "dev"),
        P(),
        P(),
        P("sub", None),
        P(None, ("dev", "sub")),
        P(None, ("dev", "sub")),
        P(("dev", "sub"), None),
        P(None, ("dev", "sub")),
        P(None, ("dev", "sub")),
        P(("groups", "dev"), None),
    )
    return jax.shard_map(
        functools.partial(body, mesh),
        mesh=mesh,
        in_specs=placed,
        out_specs=(P(("groups", "dev"), None), P(("groups", "dev"), None)),
        check_vma=False,
    )
```

```python
import functools

import jax
import jax.numpy as jnp
from jax import lax
from jax.experimental import pallas as pl
from jax.experimental.pallas import tpu as pltpu
from jax.sharding import PartitionSpec as P

CAP = 6


EPSILON = 1e-05


def expert_shard(row_block, low_rank, gate_weight, up_weight, down_weight, gate_low, up_low):
    gate_sum = jnp.dot(row_block, gate_weight, preferred_element_type=jnp.float32) + jnp.dot(
        low_rank, gate_low, preferred_element_type=jnp.float32
    )
    up_sum = jnp.dot(row_block, up_weight, preferred_element_type=jnp.float32) + jnp.dot(
        low_rank, up_low, preferred_element_type=jnp.float32
    )
    inner_act = (jax.nn.silu(gate_sum) * up_sum).astype(jnp.bfloat16)
    return jnp.dot(inner_act, down_weight, preferred_element_type=jnp.float32)


def route_gates(normed, router, experts):
    logits = jnp.dot(normed, router, preferred_element_type=jnp.float32)
    labels = lax.broadcasted_iota(jnp.int32, (1, 1, router.shape[1]), 2)
    picked = (experts[:, :, None] == labels).astype(jnp.float32)
    chosen = jnp.sum(logits[:, None, :] * picked, axis=-1)
    leading = jax.nn.sigmoid(chosen[:, 0] - chosen[:, 1])
    return jnp.stack([leading, 1.0 - leading], axis=-1)


def plain_body(
    hidden,
    query,
    cache_keys,
    cache_values,
    lengths,
    out_proj,
    norm_gain,
    router,
    low_factor,
    gate_weight,
    up_weight,
    down_weight,
    gate_low,
    up_low,
    experts,
):
    requests = hidden.shape[0]
    model_width = hidden.shape[1]
    heads_here = query.shape[1]
    kv_here = cache_keys.shape[1]
    span_len = cache_keys.shape[2]
    head_size = query.shape[2]
    grouped = query.reshape(requests, kv_here, heads_here // kv_here, head_size)
    scores = jnp.einsum(
        "rkgd,rkld->rkgl", grouped, cache_keys, preferred_element_type=jnp.float32
    ) * head_size ** (-0.5)
    visible = lax.broadcasted_iota(jnp.int32, (requests, span_len), 1) < lengths[:, None]
    scores = jnp.where(visible[:, None, None, :], scores, -1e30)
    attn_probs = jax.nn.softmax(scores, axis=-1).astype(jnp.bfloat16)
    attended = jnp.einsum(
        "rkgl,rkld->rkgd", attn_probs, cache_values, preferred_element_type=jnp.float32
    )
    attended = attended.astype(jnp.bfloat16).reshape(requests, heads_here * head_size)
    columns = jnp.dot(
        lax.all_gather(attended, "dev", axis=0, tiled=True),
        out_proj,
        preferred_element_type=jnp.float32,
    )
    partial_proj = lax.all_to_all(columns, "dev", split_axis=0, concat_axis=1, tiled=True)
    residual = hidden.astype(jnp.float32) + lax.psum(partial_proj, "sub")
    inverse = lax.rsqrt(jnp.mean(residual * residual, axis=-1, keepdims=True) + EPSILON)
    normed = (residual * inverse * norm_gain).astype(jnp.bfloat16)
    half_width = low_factor.shape[0]
    normed_half = lax.dynamic_slice_in_dim(
        normed, lax.axis_index("sub") * half_width, half_width, 1
    )
    low_partial = jnp.dot(normed_half, low_factor, preferred_element_type=jnp.float32)
    low_rank = lax.psum(low_partial, "sub").astype(jnp.bfloat16)
    rank_width = low_rank.shape[1]
    expert_count = router.shape[1]
    holders = lax.axis_size("dev") // expert_count
    gate_pair = route_gates(normed, router, experts)
    flat_ids = experts.reshape(-1)
    entries = flat_ids.shape[0]
    same_expert = flat_ids[:, None] == flat_ids[None, :]
    earlier = lax.broadcasted_iota(jnp.int32, (entries, entries), 0) > lax.broadcasted_iota(
        jnp.int32, (entries, entries), 1
    )
    slot_index = jnp.sum((same_expert & earlier).astype(jnp.int32), axis=1).reshape(requests, 2)
    target = experts * CAP + slot_index
    placement = (
        target[:, :, None] == lax.broadcasted_iota(jnp.int32, (1, 1, expert_count * CAP), 2)
    ).astype(jnp.float32)
    chosen = jnp.sum(placement, axis=1).astype(jnp.bfloat16)
    packed_rows = jnp.einsum(
        "rs,rd->sd", chosen, normed, preferred_element_type=jnp.float32
    ).astype(jnp.bfloat16)
    packed_low = jnp.einsum(
        "rs,rd->sd", chosen, low_rank, preferred_element_type=jnp.float32
    ).astype(jnp.bfloat16)
    send_rows = jnp.repeat(packed_rows.reshape(expert_count, CAP, model_width), holders, axis=0)
    send_low = jnp.repeat(packed_low.reshape(expert_count, CAP, rank_width), holders, axis=0)
    got_rows = lax.all_to_all(send_rows, "dev", split_axis=0, concat_axis=0, tiled=True)
    got_low = lax.all_to_all(send_low, "dev", split_axis=0, concat_axis=0, tiled=True)
    sources = got_rows.shape[0]
    slot_count = got_rows.shape[1]
    result = expert_shard(
        got_rows.reshape(sources * slot_count, model_width),
        got_low.reshape(sources * slot_count, rank_width),
        gate_weight,
        up_weight,
        down_weight,
        gate_low,
        up_low,
    )
    partials = result.reshape(sources, slot_count, model_width)
    returned = lax.all_to_all(
        partials.astype(jnp.bfloat16), "dev", split_axis=0, concat_axis=0, tiled=True
    ).astype(partials.dtype)
    per_slot = jnp.sum(returned.reshape(expert_count, holders, CAP, model_width), axis=1).reshape(
        expert_count * CAP, model_width
    )
    weighted = jnp.sum(placement * gate_pair[:, :, None], axis=1)
    mixture_part = jnp.dot(weighted, per_slot, precision=lax.Precision.HIGHEST)
    mixture = lax.psum(mixture_part.astype(jnp.bfloat16), "sub").astype(jnp.float32)
    return ((residual + mixture).astype(jnp.bfloat16), mixture)


CHUNK = 512
NEAR = 2
FAR_ORDER = (2, 3, 1)
FAR_STEPS = (1, 3, 2)
GATE_SLOTS = 15
GATE_COLS = 512
SPLIT = 3
VMEM_BYTES = 66 * 10**6
F32 = jnp.float32
BF16 = jnp.bfloat16


def layer_kernel(
    devs,
    subs,
    gate_slots,
    hidden,
    query,
    keys,
    values,
    lengths,
    out_proj,
    gain_hbm,
    router_hbm,
    low_factor,
    gate_w,
    up_w,
    down_w,
    gate_low,
    up_low,
    experts,
    residual,
    mixture,
    ring,
    gain,
    router,
    hid_v,
    q_v,
    k_v,
    v_v,
    op_v,
    lf_v,
    gl_v,
    ul_v,
    att_h,
    att_all,
    hid_all,
    pair_send,
    pair_recv,
    res_all,
    x_v,
    sq_v,
    low_v,
    logit_v,
    acc,
    inner,
    dsend,
    drecv,
    kept_v,
    rsend,
    rrecv,
    pack_v,
    pick_v,
    load_sem,
    a_sem,
    b_sem,
    csend_sem,
    crecv_sem,
    asend_sem,
    arecv_sem,
    gsend_sem,
    grecv_sem,
    fsend_sem,
    frecv_sem,
    psend_sem,
    precv_sem,
    xsend_sem,
    xrecv_sem,
    rs_sem,
    rr_sem,
    msend_sem,
    mrecv_sem,
):
    me = lax.axis_index("dev")
    s = lax.axis_index("sub")
    mate = 1 - s
    rows, width = hidden.shape
    all_rows = devs * rows
    heads = query.shape[1]
    kv_here, span, hd = keys.shape[1:]
    per_kv = heads // kv_here
    att_width = heads * hd
    cols = out_proj.shape[1]
    part = cols // subs
    units = gate_w.shape[1]
    half = low_factor.shape[0]
    steps = width // (2 * CHUNK)
    gate_chunks = 2 * devs

    far = devs // NEAR
    z = me // NEAR
    y = lax.rem(me, NEAR)
    beside = me + 1 - 2 * y

    def far_z(k):
        if k == 1:
            return z + 1 - 2 * lax.rem(z, 2)
        if k == 2:
            return lax.rem(z + 2, far)
        return far - 1 - z

    def far_peer(k):
        return far_z(k) * NEAR + y

    def far_beside(k):
        return far_z(k) * NEAR + 1 - y

    def peer(k):
        return lax.rem(me + k, devs)

    def remote(src, dst, send_sem, recv_sem, d, sub):
        return pltpu.make_async_remote_copy(
            src_ref=src,
            dst_ref=dst,
            send_sem=send_sem,
            recv_sem=recv_sem,
            device_id={"dev": d, "sub": sub},
            device_id_type=pl.DeviceIdType.MESH,
        )

    barrier = pltpu.get_barrier_semaphore()
    for k in range(1, devs):
        pl.semaphore_signal(
            barrier, inc=1, device_id={"dev": peer(k), "sub": s}, device_id_type=pl.DeviceIdType.MESH
        )
    pl.semaphore_signal(
        barrier, inc=1, device_id={"dev": me, "sub": mate}, device_id_type=pl.DeviceIdType.MESH
    )

    loads = [
        pltpu.make_async_copy(src, dst, load_sem.at[n])
        for n, (src, dst) in enumerate(
            [
                (query, q_v),
                (keys, k_v),
                (values, v_v),
                (hidden, hid_v),
                (low_factor, lf_v.at[s]),
                (out_proj, op_v),
                (gate_low, gl_v),
                (up_low, ul_v),
                (gain_hbm, gain),
                (router_hbm, router),
            ]
        )
    ]
    for load in loads:
        load.start()

    def block_at(k):
        kz = jnp.where(k < 2, 0, lax.rem(k - 2, far - 1) + 1)
        beside_too = jnp.where(k < 2, k, jnp.where(k < far + 1, 0, 1))
        zz = z
        for n, f in enumerate(FAR_STEPS):
            zz = jnp.where(kz == n + 1, far_z(f), zz)
        return zz * NEAR + lax.rem(y + beside_too, NEAR)

    group_cols = units
    groups = width // group_cols
    sub_rows = cols // SPLIT
    per_group = units // sub_rows
    down_base = gate_chunks * SPLIT - gate_slots * SPLIT

    def start_a(i):
        slot = lax.rem(i, gate_slots)
        at_rows = pl.ds(pl.multiple_of(block_at(i // 2) * cols, cols), cols)
        to_rows = pl.ds(pl.multiple_of(slot * cols, cols), cols)

        @pl.when(lax.rem(i, 2) == 0)
        def _():
            pltpu.make_async_copy(gate_w.at[at_rows], ring.at[to_rows], a_sem.at[slot]).start()

        @pl.when(lax.rem(i, 2) == 1)
        def _():
            pltpu.make_async_copy(up_w.at[at_rows], ring.at[to_rows], a_sem.at[slot]).start()

    def start_down(t):
        g = t // per_group
        at_rows = pl.ds(pl.multiple_of(lax.rem(t, per_group) * sub_rows, sub_rows), sub_rows)
        at_cols = pl.ds(pl.multiple_of(g * group_cols, 128), group_cols)
        to_rows = pl.ds(pl.multiple_of((down_base + t) * sub_rows, sub_rows), sub_rows)
        pltpu.make_async_copy(down_w.at[at_rows, at_cols], ring.at[to_rows], b_sem.at[g]).start()

    def refill(i):
        @pl.when(i + gate_slots < gate_chunks)
        def _():
            start_a(i + gate_slots)

        for t in range(SPLIT):
            at = (i + gate_slots - gate_chunks) * SPLIT + t

            @pl.when((at >= 0) & (at < groups * per_group))
            def _():
                start_down(at)

    def first_load(i, carry):
        start_a(i)
        return carry

    lax.fori_loop(0, gate_slots, first_load, 0)

    lane = lax.broadcasted_iota(jnp.int32, (rows, 128), 1)
    row = lax.broadcasted_iota(jnp.int32, (rows, 128), 0)
    named = jnp.zeros((rows, 128), jnp.int32)
    for r in range(rows):
        named = jnp.where(row == r, jnp.where(lane == 0, experts[0, r], experts[1, r]), named)
    att_all[me, :, att_width:] = named.astype(F32).astype(BF16)

    for load in loads[:3]:
        load.wait()
    at = lax.broadcasted_iota(jnp.int32, (heads, kv_here * span), 1)
    head = lax.broadcasted_iota(jnp.int32, (heads, kv_here * span), 0)
    place = jnp.where((at // span) == (head // per_kv), at % span, span)
    each = range(rows)
    scores = [
        lax.dot_general(
            q_v[r],
            k_v[r].reshape(kv_here * span, hd),
            (((1,), (1,)), ((), ())),
            preferred_element_type=F32,
        )
        for r in each
    ]
    scores = [jnp.where(place < lengths[r], scores[r] * hd ** (-0.5), -1e30) for r in each]
    top = [jnp.max(scores[r], axis=-1, keepdims=True) for r in each]
    grown = [jnp.exp(scores[r] - top[r]) for r in each]
    scale = [1.0 / jnp.sum(grown[r], axis=-1, keepdims=True) for r in each]
    probs = [(grown[r] * scale[r]).astype(BF16) for r in each]
    mixed = [
        jnp.dot(probs[r], v_v[r].reshape(kv_here * span, hd), preferred_element_type=F32)
        for r in each
    ]
    for r in each:
        att_h[:, r, :] = mixed[r]
    for h in range(heads):
        att_all[me, :, h * hd : (h + 1) * hd] = att_h[h].astype(BF16)
    loads[3].wait()
    mine = pl.multiple_of(me * cols + s * part, 128)
    hid_all[me] = hid_v[:, pl.ds(mine, part)]

    pl.semaphore_wait(barrier, devs)

    def gather_start(buf, index, send_sem, recv_sem):
        block = buf.at[index(me)]
        out = []
        for k in FAR_ORDER:
            out.append(remote(block, block, send_sem.at[k], recv_sem.at[me], far_peer(k), s))
        out.append(remote(block, block, send_sem.at[far], recv_sem.at[me], beside, s))
        for copy in out:
            copy.start()
        return out

    def arrived(buf, index, recv_sem, p):
        block = buf.at[index(p)]
        remote(block, block, recv_sem.at[p], recv_sem.at[p], p, s).wait_recv()

    def relay(buf, index, send_sem, recv_sem, k):
        p = far_peer(k)
        arrived(buf, index, recv_sem, p)
        block = buf.at[index(p)]
        copy = remote(block, block, send_sem.at[far + k], recv_sem.at[p], beside, s)
        copy.start()
        return copy

    same = lambda p: p
    sends = gather_start(att_all, same, asend_sem, arecv_sem)
    for k in range(1, devs):
        p = peer(k)
        theirs = pl.multiple_of(p * cols + s * part, 128)
        copy = remote(
            hid_v.at[:, pl.ds(theirs, part)],
            hid_all.at[me],
            csend_sem.at[0],
            crecv_sem.at[0],
            p,
            s,
        )
        copy.start()
    loads[4].wait()
    low_copy = remote(lf_v.at[s], lf_v.at[s], psend_sem.at[1], precv_sem.at[1], me, mate)
    low_copy.start()
    sends.append(low_copy)
    for k in FAR_STEPS:
        sends.append(relay(att_all, same, asend_sem, arecv_sem, k))
    loads[5].wait()
    hidden_copies = remote(
        hid_all.at[pl.ds(0, devs - 1)],
        hid_all.at[pl.ds(0, devs - 1)],
        csend_sem.at[0],
        crecv_sem.at[0],
        beside,
        s,
    )
    hidden_copies.wait_recv()
    sends.append(hidden_copies)
    own_hidden = jnp.concatenate([hid_all[d].astype(F32) for d in range(devs)], axis=0)
    arrived(att_all, same, arecv_sem, beside)
    for k in FAR_STEPS:
        arrived(att_all, same, arecv_sem, far_beside(k))
    attended = jnp.concatenate(
        [att_all[d, :, :att_width].astype(F32) for d in range(devs)], axis=0
    ).astype(BF16)

    theirs = pl.multiple_of(mate * part, 128)
    pair_send[...] = jnp.dot(
        attended, op_v[:, pl.ds(theirs, part)], preferred_element_type=F32
    )
    pair_copy = remote(pair_send, pair_recv, psend_sem.at[0], precv_sem.at[0], me, mate)
    pair_copy.start()
    sends.append(pair_copy)
    ours = pl.multiple_of(s * part, 128)
    projected = own_hidden + jnp.dot(
        attended, op_v[:, pl.ds(ours, part)], preferred_element_type=F32
    )
    pair_copy.wait_recv()

    def block_of(p):
        return p * subs + s

    res_all[block_of(me)] = (projected + pair_recv[...]).astype(BF16)
    own_block = res_all.at[block_of(me)]
    for k in range(1, devs):
        copy = remote(
            own_block, own_block, gsend_sem.at[k], grecv_sem.at[me], block_at(jnp.int32(k)), s
        )
        copy.start()
        sends.append(copy)

    def over(p, k):
        block = res_all.at[block_of(p)]
        copy = remote(block, block, fsend_sem.at[k], frecv_sem.at[p], me, mate)
        copy.start()
        return copy

    sends.append(over(me, 0))
    sq_v[...] = jnp.zeros_like(sq_v)
    low_v[...] = jnp.zeros_like(low_v)
    logit_v[...] = jnp.zeros_like(logit_v)
    acc[...] = jnp.zeros_like(acc)
    low_copy.wait_recv()

    def await_a(i):
        slot = lax.rem(i, gate_slots)
        at_rows = pl.ds(pl.multiple_of(slot * cols, cols), cols)
        pltpu.make_async_copy(
            gate_w.at[pl.ds(0, cols)], ring.at[at_rows], a_sem.at[slot]
        ).wait()
        return at_rows

    def arrive_next(k):
        @pl.when(k < devs - 1)
        def _():
            p = block_at(k + 1)
            arrived(res_all, block_of, grecv_sem, p)
            over(p, k + 1)

    count = router.shape[0]
    holders = devs // count
    here = me // holders
    spare = rows - CAP
    folds = CAP // spare
    main_cols = CHUNK * CAP // rows
    fold_cols = CHUNK - main_cols
    named = jnp.concatenate(
        [att_all[d, :, att_width:].astype(F32) for d in range(devs)], axis=0
    ).astype(jnp.int32)
    e0 = named[:, 0:1]
    e1 = named[:, 1:2]
    source = lax.broadcasted_iota(jnp.int32, (all_rows, all_rows), 0)
    target = lax.broadcasted_iota(jnp.int32, (all_rows, all_rows), 1)
    together = source // rows == target // rows
    names_here = jnp.where((e0 == here) | (e1 == here), 1.0, 0.0)
    slot_of = jnp.dot(
        jnp.where(together & (target < source), 1.0, 0.0).astype(BF16),
        (names_here + jnp.zeros((all_rows, all_rows), F32)).astype(BF16),
        preferred_element_type=F32,
    )
    placed = together & (slot_of == (target % rows).astype(F32))
    pack = jnp.where(placed, names_here, 0.0).T.astype(BF16)

    own_row = lax.broadcasted_iota(jnp.int32, (rows, all_rows), 0)
    lane_at = lax.broadcasted_iota(jnp.int32, (rows, all_rows), 1)
    lane_expert = lane_at // (rows * holders)
    lane_slot = lane_at % rows
    first = jnp.zeros((rows, all_rows), jnp.bool_)
    second = jnp.zeros((rows, all_rows), jnp.bool_)
    own_slot = jnp.zeros((rows, all_rows), jnp.int32)
    for r in range(rows):
        is_first = lane_expert == experts[0, r]
        is_second = lane_expert == experts[1, r]
        first = first | ((own_row == r) & is_first)
        second = second | ((own_row == r) & is_second)
        own_slot = own_slot + jnp.where((own_row > r) & (is_first | is_second), 1, 0)

    def picks(match):
        return jnp.concatenate(
            [jnp.where(first & match, 1.0, 0.0), jnp.where(second & match, 1.0, 0.0)], axis=0
        ).astype(BF16)

    pick_v[0] = picks(own_slot == lane_slot)
    for j in range(folds):
        match = jnp.zeros((rows, all_rows), jnp.bool_)
        for t in range(spare):
            match = match | ((lane_slot == CAP + t) & (own_slot == t * folds + j))
        pick_v[1 + j] = picks(match)
    pack_v[...] = pack

    per_half = half // cols
    loads[6].wait()
    loads[7].wait()
    loads[8].wait()
    loads[9].wait()

    def gate_step(k, carry):
        p = block_at(k)
        block = res_all.at[p * subs + mate]
        remote(block, block, frecv_sem.at[p], frecv_sem.at[p], me, mate).wait_recv()
        weights = await_a(2 * k)
        squares = sq_v[...]
        pieces = []
        for b in range(subs):
            r = res_all[p * subs + b].astype(F32)
            at_cols = pl.ds(pl.multiple_of(p * cols + b * part, 128), part)
            pieces.append((r * gain[:, at_cols]).astype(BF16))
            for c in range(part // 128):
                v = r[:, c * 128 : (c + 1) * 128]
                squares = squares + v * v
        sq_v[...] = squares
        x = jnp.concatenate(pieces, axis=1)
        x_v[...] = x
        at_rows = pl.ds(pl.multiple_of(lax.rem(p, per_half) * cols, cols), cols)
        at_cols = pl.ds(pl.multiple_of(p * cols, 128), cols)
        for n in range(0, units, GATE_COLS):
            acc[0, :, n : n + GATE_COLS] += jnp.dot(
                x, ring[weights, n : n + GATE_COLS], preferred_element_type=F32
            )
        low_v[...] += jnp.dot(x, lf_v[p // per_half, at_rows, :], preferred_element_type=F32)
        logit_v[...] += lax.dot_general(
            x, router[:, at_cols], (((1,), (1,)), ((), ())), preferred_element_type=F32
        )
        refill(2 * k)
        arrive_next(k)
        weights = await_a(2 * k + 1)
        x = x_v[...]
        for n in range(0, units, GATE_COLS):
            acc[1, :, n : n + GATE_COLS] += jnp.dot(
                x, ring[weights, n : n + GATE_COLS], preferred_element_type=F32
            )
        refill(2 * k + 1)
        return carry

    lax.fori_loop(0, devs, gate_step, 0)

    inverse = lax.rsqrt(jnp.sum(sq_v[...], axis=-1, keepdims=True) / width + EPSILON)
    low = (low_v[...] * inverse).astype(BF16)
    spans = [slice(n * CHUNK, (n + 1) * CHUNK) for n in range(units // CHUNK)]
    gate_low_part = [jnp.dot(low, gl_v[:, u], preferred_element_type=F32) for u in spans]
    up_low_part = [jnp.dot(low, ul_v[:, u], preferred_element_type=F32) for u in spans]
    acts = []
    for n, u in enumerate(spans):
        gate_sum = acc[0, :, u] * inverse + gate_low_part[n]
        up_sum = acc[1, :, u] * inverse + up_low_part[n]
        acts.append((gate_sum / (1.0 + jnp.exp(-gate_sum)) * up_sum).astype(BF16))
    packing = pack_v[...]
    packed = [jnp.dot(packing, act, preferred_element_type=F32) for act in acts]
    for n, u in enumerate(spans):
        inner[:, u] = packed[n].astype(BF16)

    pairs_in = group_cols // (2 * CHUNK)

    def down(c, whose):
        at_rows = pl.ds(
            pl.multiple_of((down_base + c // pairs_in * per_group) * sub_rows, sub_rows), units
        )
        at_cols = pl.ds(
            pl.multiple_of((2 * lax.rem(c, pairs_in) + whose) * CHUNK, CHUNK), CHUNK
        )
        return jnp.dot(inner[...], ring[at_rows, at_cols], preferred_element_type=F32)

    def await_group(c):
        @pl.when(lax.rem(c, pairs_in) == 0)
        def _():
            g = c // pairs_in
            pltpu.make_async_copy(
                down_w.at[:, pl.ds(0, group_cols)], ring.at[pl.ds(0, units)], b_sem.at[g]
            ).wait()

    def to_mate(c):
        remote(dsend.at[c], drecv.at[c], xsend_sem.at[0], xrecv_sem.at[c], me, mate).start()

    def from_mate(c):
        remote(dsend.at[c], drecv.at[c], xsend_sem.at[0], xrecv_sem.at[c], me, mate).wait_recv()

    row_of = lax.broadcasted_iota(jnp.int32, (rows, fold_cols), 0)

    def fold(c):
        total = kept_v[lax.rem(c, 2)] + drecv[c].astype(F32)
        shifts = sorted({CAP + t - t * folds - j for t in range(spare) for j in range(folds)})
        for d in range(devs):
            at_block = slice(d * rows, (d + 1) * rows)
            rest = total[at_block, main_cols:]
            turned = {shift: pltpu.roll(rest, shift, 0) for shift in shifts}
            for j in range(folds):
                block = total[at_block, j * fold_cols : (j + 1) * fold_cols]
                for t in range(spare):
                    block = jnp.where(
                        row_of == CAP + t, turned[CAP + t - t * folds - j], block
                    )
                to_lanes = pl.ds(
                    pl.multiple_of(c * main_cols + j * fold_cols, 128), fold_cols
                )
                rsend[d, :, to_lanes] = block.astype(BF16)

    def scatter(c):
        at_lanes = pl.ds(pl.multiple_of(c * main_cols, 128), main_cols)
        for k in range(1, devs):
            p = peer(k)
            remote(
                rsend.at[p, :, at_lanes],
                rrecv.at[me, :, at_lanes],
                rs_sem.at[0],
                rr_sem.at[c],
                p,
                s,
            ).start()
        rrecv[me, :, at_lanes] = rsend[me, :, at_lanes]

    for c in range(2):
        await_group(jnp.int32(c))
        dsend[c] = down(c, mate).astype(BF16)
        to_mate(c)
    kept_v[0] = down(0, s)

    def down_step(c, carry):
        from_mate(c - 1)
        await_group(c + 1)
        dsend[c + 1] = down(c + 1, mate).astype(BF16)
        fold(c - 1)
        to_mate(c + 1)
        scatter(c - 1)
        kept_v[lax.rem(c, 2)] = down(c, s)
        return carry

    lax.fori_loop(1, steps - 1, down_step, 0)
    from_mate(steps - 2)
    kept_v[(steps - 1) % 2] = down(steps - 1, s)
    fold(jnp.int32(steps - 2))
    scatter(steps - 2)
    from_mate(steps - 1)
    fold(jnp.int32(steps - 1))
    scatter(steps - 1)
    logits = logit_v[...] * inverse
    label = lax.broadcasted_iota(jnp.int32, (all_rows, count), 1)
    a = jnp.sum(jnp.where(label == e0, logits, 0.0), axis=-1, keepdims=True)
    b = jnp.sum(jnp.where(label == e1, logits, 0.0), axis=-1, keepdims=True)
    lead = jax.nn.sigmoid(a - b)
    pair_recv[:, :128] = lead + jnp.zeros((all_rows, 128), F32)
    my_rows = pl.ds(pl.multiple_of(me * rows, rows), rows)
    leading = pair_recv[my_rows, :128][:, 0:1]
    for b in range(devs * subs):
        pair_recv[...] = res_all[b].astype(F32)
        residual[:, b * part : (b + 1) * part] = pair_recv[my_rows, :]

    for copy in sends:
        copy.wait_send()
    for k in range(1, devs):
        block = res_all.at[block_of(me)]
        remote(block, block, fsend_sem.at[k], frecv_sem.at[me], me, mate).wait_send()
    remote(dsend, drecv, xsend_sem.at[0], xrecv_sem.at[0], me, mate).wait_send()

    for n in range(steps):
        least, end = n, n + 1
        others = rrecv.at[pl.ds(0, devs - 1), :, least * main_cols : end * main_cols]
        remote(others, others, rs_sem.at[0], rr_sem.at[n], beside, s).wait_recv()
        for c in range(least, end):
            from_lane = c * main_cols
            got = jnp.concatenate(
                [
                    rrecv[d, :, from_lane : from_lane + main_cols].astype(F32)
                    for d in range(devs)
                ],
                axis=0,
            ).astype(BF16)
            kept = jnp.dot(pick_v[0], got, preferred_element_type=F32)
            rest = jnp.zeros((2 * rows, fold_cols), F32)
            for j in range(folds):
                rest = rest + jnp.dot(
                    pick_v[1 + j],
                    got[:, j * fold_cols : (j + 1) * fold_cols],
                    preferred_element_type=F32,
                )
            both = jnp.concatenate([kept, rest], axis=1)
            at_cols = pl.ds(pl.multiple_of((2 * c + s) * CHUNK, CHUNK), CHUNK)
            mixture[:, at_cols] = leading * both[:rows] + (1.0 - leading) * both[rows:]
            swap = mixture.at[:, at_cols]
            remote(swap, swap, msend_sem.at[0], mrecv_sem.at[0], me, mate).start()

    others = rsend.at[pl.ds(0, devs - 1)]
    remote(others, others, rs_sem.at[0], rr_sem.at[0], beside, s).wait_send()
    swapped = mixture.at[:, pl.ds(0, width // 2)]
    remote(swapped, swapped, msend_sem.at[0], mrecv_sem.at[0], me, mate).wait()


def add_kernel(residual, mixture, layer_out, mixture_out):
    mixture_out[...] = mixture[...]
    layer_out[...] = (residual[...] + mixture[...]).astype(BF16)


def fits(mesh, shapes):
    devs, subs = mesh.shape["dev"], mesh.shape["sub"]
    hidden, query, keys, out_proj, router, gate_w, low_factor = shapes
    width = hidden[1]
    units = gate_w[1]
    cols = out_proj[1]
    return (
        subs == 2
        and devs == 4 * NEAR
        and devs * hidden[0] <= 128
        and hidden[0] == 8
        and CAP % (hidden[0] - CAP) == 0
        and CHUNK * CAP // hidden[0] % 128 == 0
        and CHUNK * CAP // hidden[0] == CAP // (hidden[0] - CAP) * (CHUNK - CHUNK * CAP // hidden[0])
        and query[2] == 128
        and cols % (128 * subs) == 0
        and cols * devs == width
        and low_factor[0] % cols == 0
        and units % CHUNK == 0
        and width % (2 * CHUNK) == 0
        and width // (2 * CHUNK) > 2
        and width // CHUNK % 2 == 0
        and devs % router[1] == 0
        and cols % (16 * SPLIT) == 0
        and units % (cols // SPLIT) == 0
        and width % units == 0
        and units % (2 * CHUNK) == 0
        and GATE_SLOTS * cols * units * 2 <= 48 * 10**6
        and GATE_SLOTS < 2 * devs
        and width // units * (units // (cols // SPLIT)) <= (2 * GATE_SLOTS - 2 * devs) * SPLIT
    )


def body(mesh, *args):
    (
        hidden,
        query,
        keys,
        values,
        lengths,
        out_proj,
        gain,
        router,
        low_factor,
        gate_w,
        up_w,
        down_w,
        gate_low,
        up_low,
        experts,
    ) = args
    shapes = [x.shape for x in (hidden, query, keys, out_proj, router, gate_w, low_factor)]
    if not fits(mesh, shapes):
        return plain_body(*args)
    devs, subs = mesh.shape["dev"], mesh.shape["sub"]
    rows, width = hidden.shape
    all_rows = devs * rows
    heads, hd = query.shape[1:]
    cols = out_proj.shape[1]
    part = cols // subs
    units = gate_w.shape[1]
    half, rank = low_factor.shape
    steps = width // (2 * CHUNK)
    anywhere = pl.BlockSpec(memory_space=pl.ANY)
    vmem = pl.BlockSpec(memory_space=pltpu.VMEM)
    smem = pl.BlockSpec(memory_space=pltpu.SMEM)
    dma = pltpu.SemaphoreType.DMA
    scratch = [
        pltpu.VMEM((GATE_SLOTS * cols, units), BF16),
        pltpu.VMEM((1, width), F32),
        pltpu.VMEM((router.shape[1], width), BF16),
        pltpu.VMEM(hidden.shape, BF16),
        pltpu.VMEM(query.shape, BF16),
        pltpu.VMEM(keys.shape, BF16),
        pltpu.VMEM(values.shape, BF16),
        pltpu.VMEM(out_proj.shape, BF16),
        pltpu.VMEM((subs, half, rank), BF16),
        pltpu.VMEM(gate_low.shape, BF16),
        pltpu.VMEM(up_low.shape, BF16),
        pltpu.VMEM((heads, rows, hd), F32),
        pltpu.VMEM((devs, rows, heads * hd + 128), BF16),
        pltpu.VMEM((devs, rows, part), BF16),
        pltpu.VMEM((all_rows, part), F32),
        pltpu.VMEM((all_rows, part), F32),
        pltpu.VMEM((devs * subs, all_rows, part), BF16),
        pltpu.VMEM((all_rows, cols), BF16),
        pltpu.VMEM((all_rows, 128), F32),
        pltpu.VMEM((all_rows, rank), F32),
        pltpu.VMEM((all_rows, router.shape[1]), F32),
        pltpu.VMEM((2, all_rows, units), F32),
        pltpu.VMEM((all_rows, units), BF16),
        pltpu.VMEM((steps, all_rows, CHUNK), BF16),
        pltpu.VMEM((steps, all_rows, CHUNK), BF16),
        pltpu.VMEM((2, all_rows, CHUNK), F32),
        pltpu.VMEM((devs, rows, steps * CHUNK * CAP // rows), BF16),
        pltpu.VMEM((devs, rows, steps * CHUNK * CAP // rows), BF16),
        pltpu.VMEM((all_rows, all_rows), BF16),
        pltpu.VMEM((1 + CAP // (rows - CAP), 2 * rows, all_rows), BF16),
        dma((10,)),
        dma((GATE_SLOTS,)),
        dma((width // units,)),
    ]
    scratch += [dma((devs,)) for _ in range(8)]
    scratch += [dma((2,)), dma((2,)), dma((1,)), dma((steps,))]
    scratch += [dma((1,)), dma((steps,)), dma((1,)), dma((1,))]
    residual, mixture = pl.pallas_call(
        functools.partial(layer_kernel, devs, subs, GATE_SLOTS),
        out_shape=(
            jax.ShapeDtypeStruct((rows, width), F32),
            jax.ShapeDtypeStruct((rows, width), F32),
        ),
        in_specs=[anywhere] * 4
        + [smem]
        + [anywhere] * 9
        + [smem],
        out_specs=(vmem, vmem),
        scratch_shapes=scratch,
        compiler_params=pltpu.CompilerParams(
            collective_id=0, has_side_effects=True, vmem_limit_bytes=VMEM_BYTES
        ),
    )(
        hidden,
        query,
        keys,
        values,
        lengths,
        out_proj,
        gain.reshape(1, width),
        router.T,
        low_factor,
        gate_w,
        up_w,
        down_w,
        gate_low,
        up_low,
        experts.T,
    )
    return pl.pallas_call(
        add_kernel,
        out_shape=(
            jax.ShapeDtypeStruct((rows, width), BF16),
            jax.ShapeDtypeStruct((rows, width), F32),
        ),
        in_specs=[vmem, vmem],
        out_specs=(vmem, vmem),
    )(residual, mixture)


def solution(mesh):
    placed = (
        P(("groups", "dev"), None),
        P(("groups", "dev"), "sub", None),
        P(("groups", "dev"), "sub", None, None),
        P(("groups", "dev"), "sub", None, None),
        P(("groups", "dev")),
        P("sub", "dev"),
        P(),
        P(),
        P("sub", None),
        P(None, ("dev", "sub")),
        P(None, ("dev", "sub")),
        P(("dev", "sub"), None),
        P(None, ("dev", "sub")),
        P(None, ("dev", "sub")),
        P(("groups", "dev"), None),
    )
    return jax.shard_map(
        functools.partial(body, mesh),
        mesh=mesh,
        in_specs=placed,
        out_specs=(P(("groups", "dev"), None), P(("groups", "dev"), None)),
        check_vma=False,
    )
```

```python
import functools

import jax
import jax.numpy as jnp
from jax import lax
from jax.experimental import pallas as pl
from jax.experimental.pallas import tpu as pltpu
from jax.sharding import PartitionSpec as P

CAP = 6


EPSILON = 1e-05


def expert_shard(row_block, low_rank, gate_weight, up_weight, down_weight, gate_low, up_low):
    gate_sum = jnp.dot(row_block, gate_weight, preferred_element_type=jnp.float32) + jnp.dot(
        low_rank, gate_low, preferred_element_type=jnp.float32
    )
    up_sum = jnp.dot(row_block, up_weight, preferred_element_type=jnp.float32) + jnp.dot(
        low_rank, up_low, preferred_element_type=jnp.float32
    )
    inner_act = (jax.nn.silu(gate_sum) * up_sum).astype(jnp.bfloat16)
    return jnp.dot(inner_act, down_weight, preferred_element_type=jnp.float32)


def route_gates(normed, router, experts):
    logits = jnp.dot(normed, router, preferred_element_type=jnp.float32)
    labels = lax.broadcasted_iota(jnp.int32, (1, 1, router.shape[1]), 2)
    picked = (experts[:, :, None] == labels).astype(jnp.float32)
    chosen = jnp.sum(logits[:, None, :] * picked, axis=-1)
    leading = jax.nn.sigmoid(chosen[:, 0] - chosen[:, 1])
    return jnp.stack([leading, 1.0 - leading], axis=-1)


def plain_body(
    hidden,
    query,
    cache_keys,
    cache_values,
    lengths,
    out_proj,
    norm_gain,
    router,
    low_factor,
    gate_weight,
    up_weight,
    down_weight,
    gate_low,
    up_low,
    experts,
):
    requests = hidden.shape[0]
    model_width = hidden.shape[1]
    heads_here = query.shape[1]
    kv_here = cache_keys.shape[1]
    span_len = cache_keys.shape[2]
    head_size = query.shape[2]
    grouped = query.reshape(requests, kv_here, heads_here // kv_here, head_size)
    scores = jnp.einsum(
        "rkgd,rkld->rkgl", grouped, cache_keys, preferred_element_type=jnp.float32
    ) * head_size ** (-0.5)
    visible = lax.broadcasted_iota(jnp.int32, (requests, span_len), 1) < lengths[:, None]
    scores = jnp.where(visible[:, None, None, :], scores, -1e30)
    attn_probs = jax.nn.softmax(scores, axis=-1).astype(jnp.bfloat16)
    attended = jnp.einsum(
        "rkgl,rkld->rkgd", attn_probs, cache_values, preferred_element_type=jnp.float32
    )
    attended = attended.astype(jnp.bfloat16).reshape(requests, heads_here * head_size)
    columns = jnp.dot(
        lax.all_gather(attended, "dev", axis=0, tiled=True),
        out_proj,
        preferred_element_type=jnp.float32,
    )
    partial_proj = lax.all_to_all(columns, "dev", split_axis=0, concat_axis=1, tiled=True)
    residual = hidden.astype(jnp.float32) + lax.psum(partial_proj, "sub")
    inverse = lax.rsqrt(jnp.mean(residual * residual, axis=-1, keepdims=True) + EPSILON)
    normed = (residual * inverse * norm_gain).astype(jnp.bfloat16)
    half_width = low_factor.shape[0]
    normed_half = lax.dynamic_slice_in_dim(
        normed, lax.axis_index("sub") * half_width, half_width, 1
    )
    low_partial = jnp.dot(normed_half, low_factor, preferred_element_type=jnp.float32)
    low_rank = lax.psum(low_partial, "sub").astype(jnp.bfloat16)
    rank_width = low_rank.shape[1]
    expert_count = router.shape[1]
    holders = lax.axis_size("dev") // expert_count
    gate_pair = route_gates(normed, router, experts)
    flat_ids = experts.reshape(-1)
    entries = flat_ids.shape[0]
    same_expert = flat_ids[:, None] == flat_ids[None, :]
    earlier = lax.broadcasted_iota(jnp.int32, (entries, entries), 0) > lax.broadcasted_iota(
        jnp.int32, (entries, entries), 1
    )
    slot_index = jnp.sum((same_expert & earlier).astype(jnp.int32), axis=1).reshape(requests, 2)
    target = experts * CAP + slot_index
    placement = (
        target[:, :, None] == lax.broadcasted_iota(jnp.int32, (1, 1, expert_count * CAP), 2)
    ).astype(jnp.float32)
    chosen = jnp.sum(placement, axis=1).astype(jnp.bfloat16)
    packed_rows = jnp.einsum(
        "rs,rd->sd", chosen, normed, preferred_element_type=jnp.float32
    ).astype(jnp.bfloat16)
    packed_low = jnp.einsum(
        "rs,rd->sd", chosen, low_rank, preferred_element_type=jnp.float32
    ).astype(jnp.bfloat16)
    send_rows = jnp.repeat(packed_rows.reshape(expert_count, CAP, model_width), holders, axis=0)
    send_low = jnp.repeat(packed_low.reshape(expert_count, CAP, rank_width), holders, axis=0)
    got_rows = lax.all_to_all(send_rows, "dev", split_axis=0, concat_axis=0, tiled=True)
    got_low = lax.all_to_all(send_low, "dev", split_axis=0, concat_axis=0, tiled=True)
    sources = got_rows.shape[0]
    slot_count = got_rows.shape[1]
    result = expert_shard(
        got_rows.reshape(sources * slot_count, model_width),
        got_low.reshape(sources * slot_count, rank_width),
        gate_weight,
        up_weight,
        down_weight,
        gate_low,
        up_low,
    )
    partials = result.reshape(sources, slot_count, model_width)
    returned = lax.all_to_all(
        partials.astype(jnp.bfloat16), "dev", split_axis=0, concat_axis=0, tiled=True
    ).astype(partials.dtype)
    per_slot = jnp.sum(returned.reshape(expert_count, holders, CAP, model_width), axis=1).reshape(
        expert_count * CAP, model_width
    )
    weighted = jnp.sum(placement * gate_pair[:, :, None], axis=1)
    mixture_part = jnp.dot(weighted, per_slot, precision=lax.Precision.HIGHEST)
    mixture = lax.psum(mixture_part.astype(jnp.bfloat16), "sub").astype(jnp.float32)
    return ((residual + mixture).astype(jnp.bfloat16), mixture)


CHUNK = 512
NEAR = 2
FAR_ORDER = (2, 3, 1)
FAR_STEPS = (1, 3, 2)
GATE_SLOTS = 15
GATE_COLS = 512
SPLIT = 3
VMEM_BYTES = 66 * 10**6
F32 = jnp.float32
BF16 = jnp.bfloat16


def layer_kernel(
    devs,
    subs,
    gate_slots,
    hidden,
    query,
    keys,
    values,
    lengths,
    out_proj,
    gain_hbm,
    router_hbm,
    low_factor,
    gate_w,
    up_w,
    down_w,
    gate_low,
    up_low,
    experts,
    residual,
    mixture,
    ring,
    gain,
    router,
    hid_v,
    q_v,
    k_v,
    v_v,
    op_v,
    lf_v,
    gl_v,
    ul_v,
    att_h,
    att_all,
    hid_all,
    pair_send,
    pair_recv,
    res_all,
    x_v,
    sq_v,
    low_v,
    logit_v,
    acc,
    inner,
    dsend,
    drecv,
    kept_v,
    rsend,
    rrecv,
    pack_v,
    pick_v,
    load_sem,
    a_sem,
    b_sem,
    csend_sem,
    crecv_sem,
    asend_sem,
    arecv_sem,
    gsend_sem,
    grecv_sem,
    fsend_sem,
    frecv_sem,
    psend_sem,
    precv_sem,
    xsend_sem,
    xrecv_sem,
    rs_sem,
    rr_sem,
    msend_sem,
    mrecv_sem,
):
    me = lax.axis_index("dev")
    s = lax.axis_index("sub")
    mate = 1 - s
    rows, width = hidden.shape
    all_rows = devs * rows
    heads = query.shape[1]
    kv_here, span, hd = keys.shape[1:]
    per_kv = heads // kv_here
    att_width = heads * hd
    cols = out_proj.shape[1]
    part = cols // subs
    units = gate_w.shape[1]
    half = low_factor.shape[0]
    steps = width // (2 * CHUNK)
    gate_chunks = 2 * devs

    far = devs // NEAR
    z = me // NEAR
    y = lax.rem(me, NEAR)
    beside = me + 1 - 2 * y

    def far_z(k):
        if k == 1:
            return z + 1 - 2 * lax.rem(z, 2)
        if k == 2:
            return lax.rem(z + 2, far)
        return far - 1 - z

    def far_peer(k):
        return far_z(k) * NEAR + y

    def far_beside(k):
        return far_z(k) * NEAR + 1 - y

    def peer(k):
        return lax.rem(me + k, devs)

    def remote(src, dst, send_sem, recv_sem, d, sub):
        return pltpu.make_async_remote_copy(
            src_ref=src,
            dst_ref=dst,
            send_sem=send_sem,
            recv_sem=recv_sem,
            device_id={"dev": d, "sub": sub},
            device_id_type=pl.DeviceIdType.MESH,
        )

    barrier = pltpu.get_barrier_semaphore()
    for k in range(1, devs):
        pl.semaphore_signal(
            barrier, inc=1, device_id={"dev": peer(k), "sub": s}, device_id_type=pl.DeviceIdType.MESH
        )
    pl.semaphore_signal(
        barrier, inc=1, device_id={"dev": me, "sub": mate}, device_id_type=pl.DeviceIdType.MESH
    )

    loads = [
        pltpu.make_async_copy(src, dst, load_sem.at[n])
        for n, (src, dst) in enumerate(
            [
                (query, q_v),
                (keys, k_v),
                (values, v_v),
                (hidden, hid_v),
                (low_factor, lf_v.at[s]),
                (out_proj, op_v),
                (gate_low, gl_v),
                (up_low, ul_v),
                (gain_hbm, gain),
                (router_hbm, router),
            ]
        )
    ]
    for load in loads:
        load.start()

    def block_by(k, towards):
        kz = jnp.where(k < 2, 0, lax.rem(k - 2, far - 1) + 1)
        ky = jnp.where(k < 2, k, jnp.where(k < far + 1, 0, 1))
        zz = z
        for n, f in enumerate((1, 2, 3)):
            zz = jnp.where(kz == n + 1, far_z(f) if towards else far_z(f), zz)
        return zz * NEAR + lax.rem(y + ky, NEAR)

    def block_at(k):
        return block_by(k, False)

    def block_to(k):
        return block_by(jnp.int32(k), True)

    group_cols = units
    groups = width // group_cols
    sub_rows = cols // SPLIT
    per_group = units // sub_rows
    down_base = gate_chunks * SPLIT - gate_slots * SPLIT

    def start_a(i):
        slot = lax.rem(i, gate_slots)
        at_rows = pl.ds(pl.multiple_of(block_at(i // 2) * cols, cols), cols)
        to_rows = pl.ds(pl.multiple_of(slot * cols, cols), cols)

        @pl.when(lax.rem(i, 2) == 0)
        def _():
            pltpu.make_async_copy(gate_w.at[at_rows], ring.at[to_rows], a_sem.at[slot]).start()

        @pl.when(lax.rem(i, 2) == 1)
        def _():
            pltpu.make_async_copy(up_w.at[at_rows], ring.at[to_rows], a_sem.at[slot]).start()

    def start_down(t):
        g = t // per_group
        at_rows = pl.ds(pl.multiple_of(lax.rem(t, per_group) * sub_rows, sub_rows), sub_rows)
        at_cols = pl.ds(pl.multiple_of(g * group_cols, 128), group_cols)
        to_rows = pl.ds(pl.multiple_of((down_base + t) * sub_rows, sub_rows), sub_rows)
        pltpu.make_async_copy(down_w.at[at_rows, at_cols], ring.at[to_rows], b_sem.at[g]).start()

    def refill(i):
        @pl.when(i + gate_slots < gate_chunks)
        def _():
            start_a(i + gate_slots)

        for t in range(SPLIT):
            at = (i + gate_slots - gate_chunks) * SPLIT + t

            @pl.when((at >= 0) & (at < groups * per_group))
            def _():
                start_down(at)

    def first_load(i, carry):
        start_a(i)
        return carry

    lax.fori_loop(0, gate_slots, first_load, 0)

    lane = lax.broadcasted_iota(jnp.int32, (rows, 128), 1)
    row = lax.broadcasted_iota(jnp.int32, (rows, 128), 0)
    named = jnp.zeros((rows, 128), jnp.int32)
    for r in range(rows):
        named = jnp.where(row == r, jnp.where(lane == 0, experts[0, r], experts[1, r]), named)
    att_all[me, :, att_width:] = named.astype(F32).astype(BF16)

    for load in loads[:3]:
        load.wait()
    at = lax.broadcasted_iota(jnp.int32, (heads, kv_here * span), 1)
    head = lax.broadcasted_iota(jnp.int32, (heads, kv_here * span), 0)
    place = jnp.where((at // span) == (head // per_kv), at % span, span)
    each = range(rows)
    scores = [
        lax.dot_general(
            q_v[r],
            k_v[r].reshape(kv_here * span, hd),
            (((1,), (1,)), ((), ())),
            preferred_element_type=F32,
        )
        for r in each
    ]
    scores = [jnp.where(place < lengths[r], scores[r] * hd ** (-0.5), -1e30) for r in each]
    top = [jnp.max(scores[r], axis=-1, keepdims=True) for r in each]
    grown = [jnp.exp(scores[r] - top[r]) for r in each]
    scale = [1.0 / jnp.sum(grown[r], axis=-1, keepdims=True) for r in each]
    probs = [(grown[r] * scale[r]).astype(BF16) for r in each]
    mixed = [
        jnp.dot(probs[r], v_v[r].reshape(kv_here * span, hd), preferred_element_type=F32)
        for r in each
    ]
    for r in each:
        att_h[:, r, :] = mixed[r]
    for h in range(heads):
        att_all[me, :, h * hd : (h + 1) * hd] = att_h[h].astype(BF16)
    loads[3].wait()
    mine = pl.multiple_of(me * cols + s * part, 128)
    hid_all[me] = hid_v[:, pl.ds(mine, part)]

    pl.semaphore_wait(barrier, devs)

    def gather_start(buf, index, send_sem, recv_sem):
        block = buf.at[index(me)]
        out = []
        for k in FAR_ORDER:
            out.append(remote(block, block, send_sem.at[k], recv_sem.at[me], far_peer(k), s))
        out.append(remote(block, block, send_sem.at[far], recv_sem.at[me], beside, s))
        for copy in out:
            copy.start()
        return out

    def arrived(buf, index, recv_sem, p):
        block = buf.at[index(p)]
        remote(block, block, recv_sem.at[p], recv_sem.at[p], p, s).wait_recv()

    def relay(buf, index, send_sem, recv_sem, k):
        p = far_peer(k)
        arrived(buf, index, recv_sem, p)
        block = buf.at[index(p)]
        copy = remote(block, block, send_sem.at[far + k], recv_sem.at[p], beside, s)
        copy.start()
        return copy

    same = lambda p: p
    sends = gather_start(att_all, same, asend_sem, arecv_sem)
    for k in range(1, devs):
        p = peer(k)
        theirs = pl.multiple_of(p * cols + s * part, 128)
        copy = remote(
            hid_v.at[:, pl.ds(theirs, part)],
            hid_all.at[me],
            csend_sem.at[0],
            crecv_sem.at[0],
            p,
            s,
        )
        copy.start()
    loads[4].wait()
    low_copy = remote(lf_v.at[s], lf_v.at[s], psend_sem.at[1], precv_sem.at[1], me, mate)
    low_copy.start()
    sends.append(low_copy)
    for k in FAR_STEPS:
        sends.append(relay(att_all, same, asend_sem, arecv_sem, k))
    loads[5].wait()
    hidden_copies = remote(
        hid_all.at[pl.ds(0, devs - 1)],
        hid_all.at[pl.ds(0, devs - 1)],
        csend_sem.at[0],
        crecv_sem.at[0],
        beside,
        s,
    )
    hidden_copies.wait_recv()
    sends.append(hidden_copies)
    own_hidden = jnp.concatenate([hid_all[d].astype(F32) for d in range(devs)], axis=0)
    arrived(att_all, same, arecv_sem, beside)
    for k in FAR_STEPS:
        arrived(att_all, same, arecv_sem, far_beside(k))
    attended = jnp.concatenate(
        [att_all[d, :, :att_width].astype(F32) for d in range(devs)], axis=0
    ).astype(BF16)

    theirs = pl.multiple_of(mate * part, 128)
    pair_send[...] = jnp.dot(
        attended, op_v[:, pl.ds(theirs, part)], preferred_element_type=F32
    )
    pair_copy = remote(pair_send, pair_recv, psend_sem.at[0], precv_sem.at[0], me, mate)
    pair_copy.start()
    sends.append(pair_copy)
    ours = pl.multiple_of(s * part, 128)
    projected = own_hidden + jnp.dot(
        attended, op_v[:, pl.ds(ours, part)], preferred_element_type=F32
    )
    pair_copy.wait_recv()

    def block_of(p):
        return p * subs + s

    res_all[block_of(me)] = (projected + pair_recv[...]).astype(BF16)
    def over(p, k):
        block = res_all.at[block_of(p)]
        copy = remote(block, block, fsend_sem.at[k], frecv_sem.at[p], me, mate)
        copy.start()
        return copy

    sends.append(over(me, 0))
    own_block = res_all.at[block_of(me)]
    for k in range(1, devs):
        copy = remote(
            own_block, own_block, gsend_sem.at[k], grecv_sem.at[me], block_to(k), s
        )
        copy.start()
        sends.append(copy)

    sq_v[...] = jnp.zeros_like(sq_v)
    low_v[...] = jnp.zeros_like(low_v)
    logit_v[...] = jnp.zeros_like(logit_v)
    acc[...] = jnp.zeros_like(acc)
    low_copy.wait_recv()

    def await_a(i):
        slot = lax.rem(i, gate_slots)
        at_rows = pl.ds(pl.multiple_of(slot * cols, cols), cols)
        pltpu.make_async_copy(
            gate_w.at[pl.ds(0, cols)], ring.at[at_rows], a_sem.at[slot]
        ).wait()
        return at_rows

    def arrive_next(k):
        @pl.when(k < devs - 1)
        def _():
            p = block_at(k + 1)
            arrived(res_all, block_of, grecv_sem, p)
            over(p, k + 1)

    count = router.shape[0]
    holders = devs // count
    here = me // holders
    spare = rows - CAP
    folds = CAP // spare
    main_cols = CHUNK * CAP // rows
    fold_cols = CHUNK - main_cols
    named = jnp.concatenate(
        [att_all[d, :, att_width:].astype(F32) for d in range(devs)], axis=0
    ).astype(jnp.int32)
    e0 = named[:, 0:1]
    e1 = named[:, 1:2]
    source = lax.broadcasted_iota(jnp.int32, (all_rows, all_rows), 0)
    target = lax.broadcasted_iota(jnp.int32, (all_rows, all_rows), 1)
    together = source // rows == target // rows
    names_here = jnp.where((e0 == here) | (e1 == here), 1.0, 0.0)
    slot_of = jnp.dot(
        jnp.where(together & (target < source), 1.0, 0.0).astype(BF16),
        (names_here + jnp.zeros((all_rows, all_rows), F32)).astype(BF16),
        preferred_element_type=F32,
    )
    placed = together & (slot_of == (target % rows).astype(F32))
    pack = jnp.where(placed, names_here, 0.0).T.astype(BF16)

    own_row = lax.broadcasted_iota(jnp.int32, (rows, all_rows), 0)
    lane_at = lax.broadcasted_iota(jnp.int32, (rows, all_rows), 1)
    lane_expert = lane_at // (rows * holders)
    lane_slot = lane_at % rows
    first = jnp.zeros((rows, all_rows), jnp.bool_)
    second = jnp.zeros((rows, all_rows), jnp.bool_)
    own_slot = jnp.zeros((rows, all_rows), jnp.int32)
    for r in range(rows):
        is_first = lane_expert == experts[0, r]
        is_second = lane_expert == experts[1, r]
        first = first | ((own_row == r) & is_first)
        second = second | ((own_row == r) & is_second)
        own_slot = own_slot + jnp.where((own_row > r) & (is_first | is_second), 1, 0)

    def picks(match):
        return jnp.concatenate(
            [jnp.where(first & match, 1.0, 0.0), jnp.where(second & match, 1.0, 0.0)], axis=0
        ).astype(BF16)

    pick_v[0] = picks(own_slot == lane_slot)
    for j in range(folds):
        match = jnp.zeros((rows, all_rows), jnp.bool_)
        for t in range(spare):
            match = match | ((lane_slot == CAP + t) & (own_slot == t * folds + j))
        pick_v[1 + j] = picks(match)
    pack_v[...] = pack

    per_half = half // cols
    loads[6].wait()
    loads[7].wait()
    loads[8].wait()
    loads[9].wait()

    def gate_step(k, carry):
        p = block_at(k)
        block = res_all.at[p * subs + mate]
        remote(block, block, frecv_sem.at[p], frecv_sem.at[p], me, mate).wait_recv()
        weights = await_a(2 * k)
        squares = sq_v[...]
        pieces = []
        for b in range(subs):
            r = res_all[p * subs + b].astype(F32)
            at_cols = pl.ds(pl.multiple_of(p * cols + b * part, 128), part)
            pieces.append((r * gain[:, at_cols]).astype(BF16))
            for c in range(part // 128):
                v = r[:, c * 128 : (c + 1) * 128]
                squares = squares + v * v
        sq_v[...] = squares
        x = jnp.concatenate(pieces, axis=1)
        x_v[...] = x
        at_rows = pl.ds(pl.multiple_of(lax.rem(p, per_half) * cols, cols), cols)
        at_cols = pl.ds(pl.multiple_of(p * cols, 128), cols)
        for n in range(0, units, GATE_COLS):
            acc[0, :, n : n + GATE_COLS] += jnp.dot(
                x, ring[weights, n : n + GATE_COLS], preferred_element_type=F32
            )
        low_v[...] += jnp.dot(x, lf_v[p // per_half, at_rows, :], preferred_element_type=F32)
        logit_v[...] += lax.dot_general(
            x, router[:, at_cols], (((1,), (1,)), ((), ())), preferred_element_type=F32
        )
        refill(2 * k)
        arrive_next(k)
        weights = await_a(2 * k + 1)
        x = x_v[...]
        for n in range(0, units, GATE_COLS):
            acc[1, :, n : n + GATE_COLS] += jnp.dot(
                x, ring[weights, n : n + GATE_COLS], preferred_element_type=F32
            )
        refill(2 * k + 1)
        return carry

    lax.fori_loop(0, devs, gate_step, 0)

    inverse = lax.rsqrt(jnp.sum(sq_v[...], axis=-1, keepdims=True) / width + EPSILON)
    low = (low_v[...] * inverse).astype(BF16)
    spans = [slice(n * CHUNK, (n + 1) * CHUNK) for n in range(units // CHUNK)]
    gate_low_part = [jnp.dot(low, gl_v[:, u], preferred_element_type=F32) for u in spans]
    up_low_part = [jnp.dot(low, ul_v[:, u], preferred_element_type=F32) for u in spans]
    acts = []
    for n, u in enumerate(spans):
        gate_sum = acc[0, :, u] * inverse + gate_low_part[n]
        up_sum = acc[1, :, u] * inverse + up_low_part[n]
        acts.append((gate_sum / (1.0 + jnp.exp(-gate_sum)) * up_sum).astype(BF16))
    packing = pack_v[...]
    packed = [jnp.dot(packing, act, preferred_element_type=F32) for act in acts]
    for n, u in enumerate(spans):
        inner[:, u] = packed[n].astype(BF16)

    pairs_in = group_cols // (2 * CHUNK)

    def down(c, whose):
        at_rows = pl.ds(
            pl.multiple_of((down_base + c // pairs_in * per_group) * sub_rows, sub_rows), units
        )
        at_cols = pl.ds(
            pl.multiple_of((2 * lax.rem(c, pairs_in) + whose) * CHUNK, CHUNK), CHUNK
        )
        return jnp.dot(inner[...], ring[at_rows, at_cols], preferred_element_type=F32)

    def await_group(c):
        @pl.when(lax.rem(c, pairs_in) == 0)
        def _():
            g = c // pairs_in
            pltpu.make_async_copy(
                down_w.at[:, pl.ds(0, group_cols)], ring.at[pl.ds(0, units)], b_sem.at[g]
            ).wait()

    def to_mate(c):
        remote(dsend.at[c], drecv.at[c], xsend_sem.at[0], xrecv_sem.at[c], me, mate).start()

    def from_mate(c):
        remote(dsend.at[c], drecv.at[c], xsend_sem.at[0], xrecv_sem.at[c], me, mate).wait_recv()

    row_of = lax.broadcasted_iota(jnp.int32, (rows, fold_cols), 0)

    def fold(c):
        total = kept_v[lax.rem(c, 2)] + drecv[c].astype(F32)
        shifts = sorted({CAP + t - t * folds - j for t in range(spare) for j in range(folds)})
        for d in range(devs):
            at_block = slice(d * rows, (d + 1) * rows)
            rest = total[at_block, main_cols:]
            turned = {shift: pltpu.roll(rest, shift, 0) for shift in shifts}
            for j in range(folds):
                block = total[at_block, j * fold_cols : (j + 1) * fold_cols]
                for t in range(spare):
                    block = jnp.where(
                        row_of == CAP + t, turned[CAP + t - t * folds - j], block
                    )
                to_lanes = pl.ds(
                    pl.multiple_of(c * main_cols + j * fold_cols, 128), fold_cols
                )
                rsend[d, :, to_lanes] = block.astype(BF16)

    def scatter(c):
        at_lanes = pl.ds(pl.multiple_of(c * main_cols, 128), main_cols)
        for k in range(1, devs):
            p = peer(k)
            remote(
                rsend.at[p, :, at_lanes],
                rrecv.at[me, :, at_lanes],
                rs_sem.at[0],
                rr_sem.at[c],
                p,
                s,
            ).start()
        rrecv[me, :, at_lanes] = rsend[me, :, at_lanes]

    for c in range(2):
        await_group(jnp.int32(c))
        dsend[c] = down(c, mate).astype(BF16)
        to_mate(c)
    kept_v[0] = down(0, s)

    def down_step(c, carry):
        from_mate(c - 1)
        await_group(c + 1)
        dsend[c + 1] = down(c + 1, mate).astype(BF16)
        fold(c - 1)
        to_mate(c + 1)
        scatter(c - 1)
        kept_v[lax.rem(c, 2)] = down(c, s)
        return carry

    lax.fori_loop(1, steps - 1, down_step, 0)
    from_mate(steps - 2)
    kept_v[(steps - 1) % 2] = down(steps - 1, s)
    fold(jnp.int32(steps - 2))
    scatter(steps - 2)
    from_mate(steps - 1)
    fold(jnp.int32(steps - 1))
    scatter(steps - 1)
    logits = logit_v[...] * inverse
    label = lax.broadcasted_iota(jnp.int32, (all_rows, count), 1)
    a = jnp.sum(jnp.where(label == e0, logits, 0.0), axis=-1, keepdims=True)
    b = jnp.sum(jnp.where(label == e1, logits, 0.0), axis=-1, keepdims=True)
    lead = jax.nn.sigmoid(a - b)
    pair_recv[:, :128] = lead + jnp.zeros((all_rows, 128), F32)
    my_rows = pl.ds(pl.multiple_of(me * rows, rows), rows)
    leading = pair_recv[my_rows, :128][:, 0:1]
    for b in range(devs * subs):
        pair_recv[...] = res_all[b].astype(F32)
        residual[:, b * part : (b + 1) * part] = pair_recv[my_rows, :]

    for copy in sends:
        copy.wait_send()
    for k in range(1, devs):
        block = res_all.at[block_of(me)]
        remote(block, block, fsend_sem.at[k], frecv_sem.at[me], me, mate).wait_send()
    remote(dsend, drecv, xsend_sem.at[0], xrecv_sem.at[0], me, mate).wait_send()

    for n in range(steps):
        least, end = n, n + 1
        others = rrecv.at[pl.ds(0, devs - 1), :, least * main_cols : end * main_cols]
        remote(others, others, rs_sem.at[0], rr_sem.at[n], beside, s).wait_recv()
        for c in range(least, end):
            from_lane = c * main_cols
            got = jnp.concatenate(
                [
                    rrecv[d, :, from_lane : from_lane + main_cols].astype(F32)
                    for d in range(devs)
                ],
                axis=0,
            ).astype(BF16)
            kept = jnp.dot(pick_v[0], got, preferred_element_type=F32)
            rest = jnp.zeros((2 * rows, fold_cols), F32)
            for j in range(folds):
                rest = rest + jnp.dot(
                    pick_v[1 + j],
                    got[:, j * fold_cols : (j + 1) * fold_cols],
                    preferred_element_type=F32,
                )
            both = jnp.concatenate([kept, rest], axis=1)
            at_cols = pl.ds(pl.multiple_of((2 * c + s) * CHUNK, CHUNK), CHUNK)
            mixture[:, at_cols] = leading * both[:rows] + (1.0 - leading) * both[rows:]
            swap = mixture.at[:, at_cols]
            remote(swap, swap, msend_sem.at[0], mrecv_sem.at[0], me, mate).start()

    others = rsend.at[pl.ds(0, devs - 1)]
    remote(others, others, rs_sem.at[0], rr_sem.at[0], beside, s).wait_send()
    swapped = mixture.at[:, pl.ds(0, width // 2)]
    remote(swapped, swapped, msend_sem.at[0], mrecv_sem.at[0], me, mate).wait()


def add_kernel(residual, mixture, layer_out, mixture_out):
    mixture_out[...] = mixture[...]
    layer_out[...] = (residual[...] + mixture[...]).astype(BF16)


def fits(mesh, shapes):
    devs, subs = mesh.shape["dev"], mesh.shape["sub"]
    hidden, query, keys, out_proj, router, gate_w, low_factor = shapes
    width = hidden[1]
    units = gate_w[1]
    cols = out_proj[1]
    return (
        subs == 2
        and devs == 4 * NEAR
        and devs * hidden[0] <= 128
        and hidden[0] == 8
        and CAP % (hidden[0] - CAP) == 0
        and CHUNK * CAP // hidden[0] % 128 == 0
        and CHUNK * CAP // hidden[0] == CAP // (hidden[0] - CAP) * (CHUNK - CHUNK * CAP // hidden[0])
        and query[2] == 128
        and cols % (128 * subs) == 0
        and cols * devs == width
        and low_factor[0] % cols == 0
        and units % CHUNK == 0
        and width % (2 * CHUNK) == 0
        and width // (2 * CHUNK) > 2
        and width // CHUNK % 2 == 0
        and devs % router[1] == 0
        and cols % (16 * SPLIT) == 0
        and units % (cols // SPLIT) == 0
        and width % units == 0
        and units % (2 * CHUNK) == 0
        and GATE_SLOTS * cols * units * 2 <= 48 * 10**6
        and GATE_SLOTS < 2 * devs
        and width // units * (units // (cols // SPLIT)) <= (2 * GATE_SLOTS - 2 * devs) * SPLIT
    )


def body(mesh, *args):
    (
        hidden,
        query,
        keys,
        values,
        lengths,
        out_proj,
        gain,
        router,
        low_factor,
        gate_w,
        up_w,
        down_w,
        gate_low,
        up_low,
        experts,
    ) = args
    shapes = [x.shape for x in (hidden, query, keys, out_proj, router, gate_w, low_factor)]
    if not fits(mesh, shapes):
        return plain_body(*args)
    devs, subs = mesh.shape["dev"], mesh.shape["sub"]
    rows, width = hidden.shape
    all_rows = devs * rows
    heads, hd = query.shape[1:]
    cols = out_proj.shape[1]
    part = cols // subs
    units = gate_w.shape[1]
    half, rank = low_factor.shape
    steps = width // (2 * CHUNK)
    anywhere = pl.BlockSpec(memory_space=pl.ANY)
    vmem = pl.BlockSpec(memory_space=pltpu.VMEM)
    smem = pl.BlockSpec(memory_space=pltpu.SMEM)
    dma = pltpu.SemaphoreType.DMA
    scratch = [
        pltpu.VMEM((GATE_SLOTS * cols, units), BF16),
        pltpu.VMEM((1, width), F32),
        pltpu.VMEM((router.shape[1], width), BF16),
        pltpu.VMEM(hidden.shape, BF16),
        pltpu.VMEM(query.shape, BF16),
        pltpu.VMEM(keys.shape, BF16),
        pltpu.VMEM(values.shape, BF16),
        pltpu.VMEM(out_proj.shape, BF16),
        pltpu.VMEM((subs, half, rank), BF16),
        pltpu.VMEM(gate_low.shape, BF16),
        pltpu.VMEM(up_low.shape, BF16),
        pltpu.VMEM((heads, rows, hd), F32),
        pltpu.VMEM((devs, rows, heads * hd + 128), BF16),
        pltpu.VMEM((devs, rows, part), BF16),
        pltpu.VMEM((all_rows, part), F32),
        pltpu.VMEM((all_rows, part), F32),
        pltpu.VMEM((devs * subs, all_rows, part), BF16),
        pltpu.VMEM((all_rows, cols), BF16),
        pltpu.VMEM((all_rows, 128), F32),
        pltpu.VMEM((all_rows, rank), F32),
        pltpu.VMEM((all_rows, router.shape[1]), F32),
        pltpu.VMEM((2, all_rows, units), F32),
        pltpu.VMEM((all_rows, units), BF16),
        pltpu.VMEM((steps, all_rows, CHUNK), BF16),
        pltpu.VMEM((steps, all_rows, CHUNK), BF16),
        pltpu.VMEM((2, all_rows, CHUNK), F32),
        pltpu.VMEM((devs, rows, steps * CHUNK * CAP // rows), BF16),
        pltpu.VMEM((devs, rows, steps * CHUNK * CAP // rows), BF16),
        pltpu.VMEM((all_rows, all_rows), BF16),
        pltpu.VMEM((1 + CAP // (rows - CAP), 2 * rows, all_rows), BF16),
        dma((10,)),
        dma((GATE_SLOTS,)),
        dma((width // units,)),
    ]
    scratch += [dma((devs,)) for _ in range(8)]
    scratch += [dma((2,)), dma((2,)), dma((1,)), dma((steps,))]
    scratch += [dma((1,)), dma((steps,)), dma((1,)), dma((1,))]
    residual, mixture = pl.pallas_call(
        functools.partial(layer_kernel, devs, subs, GATE_SLOTS),
        out_shape=(
            jax.ShapeDtypeStruct((rows, width), F32),
            jax.ShapeDtypeStruct((rows, width), F32),
        ),
        in_specs=[anywhere] * 4
        + [smem]
        + [anywhere] * 9
        + [smem],
        out_specs=(vmem, vmem),
        scratch_shapes=scratch,
        compiler_params=pltpu.CompilerParams(
            collective_id=0, has_side_effects=True, vmem_limit_bytes=VMEM_BYTES
        ),
    )(
        hidden,
        query,
        keys,
        values,
        lengths,
        out_proj,
        gain.reshape(1, width),
        router.T,
        low_factor,
        gate_w,
        up_w,
        down_w,
        gate_low,
        up_low,
        experts.T,
    )
    return pl.pallas_call(
        add_kernel,
        out_shape=(
            jax.ShapeDtypeStruct((rows, width), BF16),
            jax.ShapeDtypeStruct((rows, width), F32),
        ),
        in_specs=[vmem, vmem],
        out_specs=(vmem, vmem),
    )(residual, mixture)


def solution(mesh):
    placed = (
        P(("groups", "dev"), None),
        P(("groups", "dev"), "sub", None),
        P(("groups", "dev"), "sub", None, None),
        P(("groups", "dev"), "sub", None, None),
        P(("groups", "dev")),
        P("sub", "dev"),
        P(),
        P(),
        P("sub", None),
        P(None, ("dev", "sub")),
        P(None, ("dev", "sub")),
        P(("dev", "sub"), None),
        P(None, ("dev", "sub")),
        P(None, ("dev", "sub")),
        P(("groups", "dev"), None),
    )
    return jax.shard_map(
        functools.partial(body, mesh),
        mesh=mesh,
        in_specs=placed,
        out_specs=(P(("groups", "dev"), None), P(("groups", "dev"), None)),
        check_vma=False,
    )
```

```python
import functools

import jax
import jax.numpy as jnp
from jax import lax
from jax.experimental import pallas as pl
from jax.experimental.pallas import tpu as pltpu
from jax.sharding import PartitionSpec as P

CAP = 6


EPSILON = 1e-05


def expert_shard(row_block, low_rank, gate_weight, up_weight, down_weight, gate_low, up_low):
    gate_sum = jnp.dot(row_block, gate_weight, preferred_element_type=jnp.float32) + jnp.dot(
        low_rank, gate_low, preferred_element_type=jnp.float32
    )
    up_sum = jnp.dot(row_block, up_weight, preferred_element_type=jnp.float32) + jnp.dot(
        low_rank, up_low, preferred_element_type=jnp.float32
    )
    inner_act = (jax.nn.silu(gate_sum) * up_sum).astype(jnp.bfloat16)
    return jnp.dot(inner_act, down_weight, preferred_element_type=jnp.float32)


def route_gates(normed, router, experts):
    logits = jnp.dot(normed, router, preferred_element_type=jnp.float32)
    labels = lax.broadcasted_iota(jnp.int32, (1, 1, router.shape[1]), 2)
    picked = (experts[:, :, None] == labels).astype(jnp.float32)
    chosen = jnp.sum(logits[:, None, :] * picked, axis=-1)
    leading = jax.nn.sigmoid(chosen[:, 0] - chosen[:, 1])
    return jnp.stack([leading, 1.0 - leading], axis=-1)


def plain_body(
    hidden,
    query,
    cache_keys,
    cache_values,
    lengths,
    out_proj,
    norm_gain,
    router,
    low_factor,
    gate_weight,
    up_weight,
    down_weight,
    gate_low,
    up_low,
    experts,
):
    requests = hidden.shape[0]
    model_width = hidden.shape[1]
    heads_here = query.shape[1]
    kv_here = cache_keys.shape[1]
    span_len = cache_keys.shape[2]
    head_size = query.shape[2]
    grouped = query.reshape(requests, kv_here, heads_here // kv_here, head_size)
    scores = jnp.einsum(
        "rkgd,rkld->rkgl", grouped, cache_keys, preferred_element_type=jnp.float32
    ) * head_size ** (-0.5)
    visible = lax.broadcasted_iota(jnp.int32, (requests, span_len), 1) < lengths[:, None]
    scores = jnp.where(visible[:, None, None, :], scores, -1e30)
    attn_probs = jax.nn.softmax(scores, axis=-1).astype(jnp.bfloat16)
    attended = jnp.einsum(
        "rkgl,rkld->rkgd", attn_probs, cache_values, preferred_element_type=jnp.float32
    )
    attended = attended.astype(jnp.bfloat16).reshape(requests, heads_here * head_size)
    columns = jnp.dot(
        lax.all_gather(attended, "dev", axis=0, tiled=True),
        out_proj,
        preferred_element_type=jnp.float32,
    )
    partial_proj = lax.all_to_all(columns, "dev", split_axis=0, concat_axis=1, tiled=True)
    residual = hidden.astype(jnp.float32) + lax.psum(partial_proj, "sub")
    inverse = lax.rsqrt(jnp.mean(residual * residual, axis=-1, keepdims=True) + EPSILON)
    normed = (residual * inverse * norm_gain).astype(jnp.bfloat16)
    half_width = low_factor.shape[0]
    normed_half = lax.dynamic_slice_in_dim(
        normed, lax.axis_index("sub") * half_width, half_width, 1
    )
    low_partial = jnp.dot(normed_half, low_factor, preferred_element_type=jnp.float32)
    low_rank = lax.psum(low_partial, "sub").astype(jnp.bfloat16)
    rank_width = low_rank.shape[1]
    expert_count = router.shape[1]
    holders = lax.axis_size("dev") // expert_count
    gate_pair = route_gates(normed, router, experts)
    flat_ids = experts.reshape(-1)
    entries = flat_ids.shape[0]
    same_expert = flat_ids[:, None] == flat_ids[None, :]
    earlier = lax.broadcasted_iota(jnp.int32, (entries, entries), 0) > lax.broadcasted_iota(
        jnp.int32, (entries, entries), 1
    )
    slot_index = jnp.sum((same_expert & earlier).astype(jnp.int32), axis=1).reshape(requests, 2)
    target = experts * CAP + slot_index
    placement = (
        target[:, :, None] == lax.broadcasted_iota(jnp.int32, (1, 1, expert_count * CAP), 2)
    ).astype(jnp.float32)
    chosen = jnp.sum(placement, axis=1).astype(jnp.bfloat16)
    packed_rows = jnp.einsum(
        "rs,rd->sd", chosen, normed, preferred_element_type=jnp.float32
    ).astype(jnp.bfloat16)
    packed_low = jnp.einsum(
        "rs,rd->sd", chosen, low_rank, preferred_element_type=jnp.float32
    ).astype(jnp.bfloat16)
    send_rows = jnp.repeat(packed_rows.reshape(expert_count, CAP, model_width), holders, axis=0)
    send_low = jnp.repeat(packed_low.reshape(expert_count, CAP, rank_width), holders, axis=0)
    got_rows = lax.all_to_all(send_rows, "dev", split_axis=0, concat_axis=0, tiled=True)
    got_low = lax.all_to_all(send_low, "dev", split_axis=0, concat_axis=0, tiled=True)
    sources = got_rows.shape[0]
    slot_count = got_rows.shape[1]
    result = expert_shard(
        got_rows.reshape(sources * slot_count, model_width),
        got_low.reshape(sources * slot_count, rank_width),
        gate_weight,
        up_weight,
        down_weight,
        gate_low,
        up_low,
    )
    partials = result.reshape(sources, slot_count, model_width)
    returned = lax.all_to_all(
        partials.astype(jnp.bfloat16), "dev", split_axis=0, concat_axis=0, tiled=True
    ).astype(partials.dtype)
    per_slot = jnp.sum(returned.reshape(expert_count, holders, CAP, model_width), axis=1).reshape(
        expert_count * CAP, model_width
    )
    weighted = jnp.sum(placement * gate_pair[:, :, None], axis=1)
    mixture_part = jnp.dot(weighted, per_slot, precision=lax.Precision.HIGHEST)
    mixture = lax.psum(mixture_part.astype(jnp.bfloat16), "sub").astype(jnp.float32)
    return ((residual + mixture).astype(jnp.bfloat16), mixture)


CHUNK = 512
NEAR = 2
FAR_ORDER = (2, 3, 1)
FAR_STEPS = (1, 3, 2)
GATE_SLOTS = 15
GATE_COLS = 512
SPLIT = 3
EARLY_FROM = 4
VMEM_BYTES = 66 * 10**6
F32 = jnp.float32
BF16 = jnp.bfloat16


def layer_kernel(
    devs,
    subs,
    gate_slots,
    hidden,
    query,
    keys,
    values,
    lengths,
    out_proj,
    gain_hbm,
    router_hbm,
    low_factor,
    gate_w,
    up_w,
    down_w,
    gate_low,
    up_low,
    experts,
    residual,
    mixture,
    ring,
    gain,
    router,
    hid_v,
    q_v,
    k_v,
    v_v,
    op_v,
    lf_v,
    gl_v,
    ul_v,
    att_h,
    att_all,
    hid_all,
    pair_send,
    pair_recv,
    res_all,
    x_v,
    sq_v,
    low_v,
    logit_v,
    acc,
    inner,
    dsend,
    drecv,
    kept_v,
    rsend,
    rrecv,
    pack_v,
    pick_v,
    load_sem,
    a_sem,
    b_sem,
    csend_sem,
    crecv_sem,
    asend_sem,
    arecv_sem,
    gsend_sem,
    grecv_sem,
    fsend_sem,
    frecv_sem,
    psend_sem,
    precv_sem,
    xsend_sem,
    xrecv_sem,
    rs_sem,
    rr_sem,
    msend_sem,
    mrecv_sem,
):
    me = lax.axis_index("dev")
    s = lax.axis_index("sub")
    mate = 1 - s
    rows, width = hidden.shape
    all_rows = devs * rows
    heads = query.shape[1]
    kv_here, span, hd = keys.shape[1:]
    per_kv = heads // kv_here
    att_width = heads * hd
    cols = out_proj.shape[1]
    part = cols // subs
    units = gate_w.shape[1]
    half = low_factor.shape[0]
    steps = width // (2 * CHUNK)
    gate_chunks = 2 * devs

    far = devs // NEAR
    z = me // NEAR
    y = lax.rem(me, NEAR)
    beside = me + 1 - 2 * y

    def far_z(k):
        if k == 1:
            return z + 1 - 2 * lax.rem(z, 2)
        if k == 2:
            return lax.rem(z + 2, far)
        return far - 1 - z

    def far_peer(k):
        return far_z(k) * NEAR + y

    def far_beside(k):
        return far_z(k) * NEAR + 1 - y

    def peer(k):
        return lax.rem(me + k, devs)

    def remote(src, dst, send_sem, recv_sem, d, sub):
        return pltpu.make_async_remote_copy(
            src_ref=src,
            dst_ref=dst,
            send_sem=send_sem,
            recv_sem=recv_sem,
            device_id={"dev": d, "sub": sub},
            device_id_type=pl.DeviceIdType.MESH,
        )

    barrier = pltpu.get_barrier_semaphore()
    for k in range(1, devs):
        pl.semaphore_signal(
            barrier, inc=1, device_id={"dev": peer(k), "sub": s}, device_id_type=pl.DeviceIdType.MESH
        )
    pl.semaphore_signal(
        barrier, inc=1, device_id={"dev": me, "sub": mate}, device_id_type=pl.DeviceIdType.MESH
    )

    loads = [
        pltpu.make_async_copy(src, dst, load_sem.at[n])
        for n, (src, dst) in enumerate(
            [
                (query, q_v),
                (keys, k_v),
                (values, v_v),
                (hidden, hid_v),
                (low_factor, lf_v.at[s]),
                (out_proj, op_v),
                (gate_low, gl_v),
                (up_low, ul_v),
                (gain_hbm, gain),
                (router_hbm, router),
            ]
        )
    ]
    for load in loads:
        load.start()

    def block_by(k, towards):
        kz = jnp.where(k < 2, 0, lax.rem(k - 2, far - 1) + 1)
        ky = jnp.where(k < 2, k, jnp.where(k < far + 1, 0, 1))
        zz = z
        for n, f in enumerate((1, 2, 3)):
            zz = jnp.where(kz == n + 1, far_z(f) if towards else far_z(f), zz)
        return zz * NEAR + lax.rem(y + ky, NEAR)

    def block_at(k):
        return block_by(k, False)

    def block_to(k):
        return block_by(jnp.int32(k), True)

    group_cols = units
    groups = width // group_cols
    sub_rows = cols // SPLIT
    per_group = units // sub_rows
    down_base = gate_chunks * SPLIT - gate_slots * SPLIT

    def start_a(i):
        slot = lax.rem(i, gate_slots)
        at_rows = pl.ds(pl.multiple_of(block_at(i // 2) * cols, cols), cols)
        to_rows = pl.ds(pl.multiple_of(slot * cols, cols), cols)

        @pl.when(lax.rem(i, 2) == 0)
        def _():
            pltpu.make_async_copy(gate_w.at[at_rows], ring.at[to_rows], a_sem.at[slot]).start()

        @pl.when(lax.rem(i, 2) == 1)
        def _():
            pltpu.make_async_copy(up_w.at[at_rows], ring.at[to_rows], a_sem.at[slot]).start()

    def start_down(t):
        g = t // per_group
        at_rows = pl.ds(pl.multiple_of(lax.rem(t, per_group) * sub_rows, sub_rows), sub_rows)
        at_cols = pl.ds(pl.multiple_of(g * group_cols, 128), group_cols)
        to_rows = pl.ds(pl.multiple_of((down_base + t) * sub_rows, sub_rows), sub_rows)
        pltpu.make_async_copy(down_w.at[at_rows, at_cols], ring.at[to_rows], b_sem.at[g]).start()

    def refill(i):
        @pl.when(i + gate_slots < gate_chunks)
        def _():
            start_a(i + gate_slots)

        for t in range(SPLIT):
            at = (i + gate_slots - gate_chunks) * SPLIT + t

            @pl.when((at >= 0) & (at < groups * per_group))
            def _():
                start_down(at)

    def first_load(i, carry):
        start_a(i)
        return carry

    lax.fori_loop(0, gate_slots, first_load, 0)

    lane = lax.broadcasted_iota(jnp.int32, (rows, 128), 1)
    row = lax.broadcasted_iota(jnp.int32, (rows, 128), 0)
    named = jnp.zeros((rows, 128), jnp.int32)
    for r in range(rows):
        named = jnp.where(row == r, jnp.where(lane == 0, experts[0, r], experts[1, r]), named)
    att_all[me, :, att_width:] = named.astype(F32).astype(BF16)

    for load in loads[:3]:
        load.wait()
    at = lax.broadcasted_iota(jnp.int32, (heads, kv_here * span), 1)
    head = lax.broadcasted_iota(jnp.int32, (heads, kv_here * span), 0)
    place = jnp.where((at // span) == (head // per_kv), at % span, span)
    each = range(rows)
    scores = [
        lax.dot_general(
            q_v[r],
            k_v[r].reshape(kv_here * span, hd),
            (((1,), (1,)), ((), ())),
            preferred_element_type=F32,
        )
        for r in each
    ]
    scores = [jnp.where(place < lengths[r], scores[r] * hd ** (-0.5), -1e30) for r in each]
    top = [jnp.max(scores[r], axis=-1, keepdims=True) for r in each]
    grown = [jnp.exp(scores[r] - top[r]) for r in each]
    scale = [1.0 / jnp.sum(grown[r], axis=-1, keepdims=True) for r in each]
    probs = [(grown[r] * scale[r]).astype(BF16) for r in each]
    mixed = [
        jnp.dot(probs[r], v_v[r].reshape(kv_here * span, hd), preferred_element_type=F32)
        for r in each
    ]
    for r in each:
        att_h[:, r, :] = mixed[r]
    for h in range(heads):
        att_all[me, :, h * hd : (h + 1) * hd] = att_h[h].astype(BF16)
    loads[3].wait()
    mine = pl.multiple_of(me * cols + s * part, 128)
    hid_all[me] = hid_v[:, pl.ds(mine, part)]

    pl.semaphore_wait(barrier, devs)

    def gather_start(buf, index, send_sem, recv_sem):
        block = buf.at[index(me)]
        out = []
        for k in FAR_ORDER:
            out.append(remote(block, block, send_sem.at[k], recv_sem.at[me], far_peer(k), s))
        out.append(remote(block, block, send_sem.at[far], recv_sem.at[me], beside, s))
        for copy in out:
            copy.start()
        return out

    def arrived(buf, index, recv_sem, p):
        block = buf.at[index(p)]
        remote(block, block, recv_sem.at[p], recv_sem.at[p], p, s).wait_recv()

    def relay(buf, index, send_sem, recv_sem, k):
        p = far_peer(k)
        arrived(buf, index, recv_sem, p)
        block = buf.at[index(p)]
        copy = remote(block, block, send_sem.at[far + k], recv_sem.at[p], beside, s)
        copy.start()
        return copy

    same = lambda p: p
    sends = gather_start(att_all, same, asend_sem, arecv_sem)
    for k in range(1, devs):
        p = peer(k)
        theirs = pl.multiple_of(p * cols + s * part, 128)
        copy = remote(
            hid_v.at[:, pl.ds(theirs, part)],
            hid_all.at[me],
            csend_sem.at[0],
            crecv_sem.at[0],
            p,
            s,
        )
        copy.start()
    loads[4].wait()
    low_copy = remote(lf_v.at[s], lf_v.at[s], psend_sem.at[1], precv_sem.at[1], me, mate)
    low_copy.start()
    sends.append(low_copy)
    for k in FAR_STEPS:
        sends.append(relay(att_all, same, asend_sem, arecv_sem, k))
    loads[5].wait()
    hidden_copies = remote(
        hid_all.at[pl.ds(0, devs - 1)],
        hid_all.at[pl.ds(0, devs - 1)],
        csend_sem.at[0],
        crecv_sem.at[0],
        beside,
        s,
    )
    hidden_copies.wait_recv()
    sends.append(hidden_copies)
    own_hidden = jnp.concatenate([hid_all[d].astype(F32) for d in range(devs)], axis=0)
    arrived(att_all, same, arecv_sem, beside)
    for k in FAR_STEPS:
        arrived(att_all, same, arecv_sem, far_beside(k))
    attended = jnp.concatenate(
        [att_all[d, :, :att_width].astype(F32) for d in range(devs)], axis=0
    ).astype(BF16)

    theirs = pl.multiple_of(mate * part, 128)
    pair_send[...] = jnp.dot(
        attended, op_v[:, pl.ds(theirs, part)], preferred_element_type=F32
    )
    pair_copy = remote(pair_send, pair_recv, psend_sem.at[0], precv_sem.at[0], me, mate)
    pair_copy.start()
    sends.append(pair_copy)
    ours = pl.multiple_of(s * part, 128)
    projected = own_hidden + jnp.dot(
        attended, op_v[:, pl.ds(ours, part)], preferred_element_type=F32
    )
    pair_copy.wait_recv()

    def block_of(p):
        return p * subs + s

    res_all[block_of(me)] = (projected + pair_recv[...]).astype(BF16)
    def over(p, k):
        block = res_all.at[block_of(p)]
        copy = remote(block, block, fsend_sem.at[k], frecv_sem.at[p], me, mate)
        copy.start()
        return copy

    sends.append(over(me, 0))
    own_block = res_all.at[block_of(me)]
    for k in range(1, devs):
        copy = remote(
            own_block, own_block, gsend_sem.at[k], grecv_sem.at[me], block_to(k), s
        )
        copy.start()
        sends.append(copy)

    sq_v[...] = jnp.zeros_like(sq_v)
    low_v[...] = jnp.zeros_like(low_v)
    logit_v[...] = jnp.zeros_like(logit_v)
    acc[...] = jnp.zeros_like(acc)
    low_copy.wait_recv()

    def await_a(i):
        slot = lax.rem(i, gate_slots)
        at_rows = pl.ds(pl.multiple_of(slot * cols, cols), cols)
        pltpu.make_async_copy(
            gate_w.at[pl.ds(0, cols)], ring.at[at_rows], a_sem.at[slot]
        ).wait()
        return at_rows

    def arrive_next(k, now):
        @pl.when(now & (k < devs - 1))
        def _():
            p = block_at(k + 1)
            arrived(res_all, block_of, grecv_sem, p)
            over(p, k + 1)

    count = router.shape[0]
    holders = devs // count
    here = me // holders
    spare = rows - CAP
    folds = CAP // spare
    main_cols = CHUNK * CAP // rows
    fold_cols = CHUNK - main_cols
    named = jnp.concatenate(
        [att_all[d, :, att_width:].astype(F32) for d in range(devs)], axis=0
    ).astype(jnp.int32)
    e0 = named[:, 0:1]
    e1 = named[:, 1:2]
    source = lax.broadcasted_iota(jnp.int32, (all_rows, all_rows), 0)
    target = lax.broadcasted_iota(jnp.int32, (all_rows, all_rows), 1)
    together = source // rows == target // rows
    names_here = jnp.where((e0 == here) | (e1 == here), 1.0, 0.0)
    slot_of = jnp.dot(
        jnp.where(together & (target < source), 1.0, 0.0).astype(BF16),
        (names_here + jnp.zeros((all_rows, all_rows), F32)).astype(BF16),
        preferred_element_type=F32,
    )
    placed = together & (slot_of == (target % rows).astype(F32))
    pack = jnp.where(placed, names_here, 0.0).T.astype(BF16)

    own_row = lax.broadcasted_iota(jnp.int32, (rows, all_rows), 0)
    lane_at = lax.broadcasted_iota(jnp.int32, (rows, all_rows), 1)
    lane_expert = lane_at // (rows * holders)
    lane_slot = lane_at % rows
    first = jnp.zeros((rows, all_rows), jnp.bool_)
    second = jnp.zeros((rows, all_rows), jnp.bool_)
    own_slot = jnp.zeros((rows, all_rows), jnp.int32)
    for r in range(rows):
        is_first = lane_expert == experts[0, r]
        is_second = lane_expert == experts[1, r]
        first = first | ((own_row == r) & is_first)
        second = second | ((own_row == r) & is_second)
        own_slot = own_slot + jnp.where((own_row > r) & (is_first | is_second), 1, 0)

    def picks(match):
        return jnp.concatenate(
            [jnp.where(first & match, 1.0, 0.0), jnp.where(second & match, 1.0, 0.0)], axis=0
        ).astype(BF16)

    pick_v[0] = picks(own_slot == lane_slot)
    for j in range(folds):
        match = jnp.zeros((rows, all_rows), jnp.bool_)
        for t in range(spare):
            match = match | ((lane_slot == CAP + t) & (own_slot == t * folds + j))
        pick_v[1 + j] = picks(match)
    pack_v[...] = pack

    per_half = half // cols
    loads[6].wait()
    loads[7].wait()
    loads[8].wait()
    loads[9].wait()

    def gate_step(k, carry):
        arrive_next(k, k >= EARLY_FROM)
        p = block_at(k)
        block = res_all.at[p * subs + mate]
        remote(block, block, frecv_sem.at[p], frecv_sem.at[p], me, mate).wait_recv()
        weights = await_a(2 * k)
        squares = sq_v[...]
        pieces = []
        for b in range(subs):
            r = res_all[p * subs + b].astype(F32)
            at_cols = pl.ds(pl.multiple_of(p * cols + b * part, 128), part)
            pieces.append((r * gain[:, at_cols]).astype(BF16))
            for c in range(part // 128):
                v = r[:, c * 128 : (c + 1) * 128]
                squares = squares + v * v
        sq_v[...] = squares
        x = jnp.concatenate(pieces, axis=1)
        x_v[...] = x
        at_rows = pl.ds(pl.multiple_of(lax.rem(p, per_half) * cols, cols), cols)
        at_cols = pl.ds(pl.multiple_of(p * cols, 128), cols)
        for n in range(0, units, GATE_COLS):
            acc[0, :, n : n + GATE_COLS] += jnp.dot(
                x, ring[weights, n : n + GATE_COLS], preferred_element_type=F32
            )
        low_v[...] += jnp.dot(x, lf_v[p // per_half, at_rows, :], preferred_element_type=F32)
        logit_v[...] += lax.dot_general(
            x, router[:, at_cols], (((1,), (1,)), ((), ())), preferred_element_type=F32
        )
        refill(2 * k)
        arrive_next(k, k < EARLY_FROM)
        weights = await_a(2 * k + 1)
        x = x_v[...]
        for n in range(0, units, GATE_COLS):
            acc[1, :, n : n + GATE_COLS] += jnp.dot(
                x, ring[weights, n : n + GATE_COLS], preferred_element_type=F32
            )
        refill(2 * k + 1)
        return carry

    lax.fori_loop(0, devs, gate_step, 0)

    inverse = lax.rsqrt(jnp.sum(sq_v[...], axis=-1, keepdims=True) / width + EPSILON)
    low = (low_v[...] * inverse).astype(BF16)
    spans = [slice(n * CHUNK, (n + 1) * CHUNK) for n in range(units // CHUNK)]
    gate_low_part = [jnp.dot(low, gl_v[:, u], preferred_element_type=F32) for u in spans]
    up_low_part = [jnp.dot(low, ul_v[:, u], preferred_element_type=F32) for u in spans]
    acts = []
    for n, u in enumerate(spans):
        gate_sum = acc[0, :, u] * inverse + gate_low_part[n]
        up_sum = acc[1, :, u] * inverse + up_low_part[n]
        acts.append((gate_sum / (1.0 + jnp.exp(-gate_sum)) * up_sum).astype(BF16))
    packing = pack_v[...]
    packed = [jnp.dot(packing, act, preferred_element_type=F32) for act in acts]
    for n, u in enumerate(spans):
        inner[:, u] = packed[n].astype(BF16)

    pairs_in = group_cols // (2 * CHUNK)

    def down(c, whose):
        at_rows = pl.ds(
            pl.multiple_of((down_base + c // pairs_in * per_group) * sub_rows, sub_rows), units
        )
        at_cols = pl.ds(
            pl.multiple_of((2 * lax.rem(c, pairs_in) + whose) * CHUNK, CHUNK), CHUNK
        )
        return jnp.dot(inner[...], ring[at_rows, at_cols], preferred_element_type=F32)

    def await_group(c):
        @pl.when(lax.rem(c, pairs_in) == 0)
        def _():
            g = c // pairs_in
            pltpu.make_async_copy(
                down_w.at[:, pl.ds(0, group_cols)], ring.at[pl.ds(0, units)], b_sem.at[g]
            ).wait()

    def to_mate(c):
        remote(dsend.at[c], drecv.at[c], xsend_sem.at[0], xrecv_sem.at[c], me, mate).start()

    def from_mate(c):
        remote(dsend.at[c], drecv.at[c], xsend_sem.at[0], xrecv_sem.at[c], me, mate).wait_recv()

    row_of = lax.broadcasted_iota(jnp.int32, (rows, fold_cols), 0)

    def fold(c):
        total = kept_v[lax.rem(c, 2)] + drecv[c].astype(F32)
        shifts = sorted({CAP + t - t * folds - j for t in range(spare) for j in range(folds)})
        for d in range(devs):
            at_block = slice(d * rows, (d + 1) * rows)
            rest = total[at_block, main_cols:]
            turned = {shift: pltpu.roll(rest, shift, 0) for shift in shifts}
            for j in range(folds):
                block = total[at_block, j * fold_cols : (j + 1) * fold_cols]
                for t in range(spare):
                    block = jnp.where(
                        row_of == CAP + t, turned[CAP + t - t * folds - j], block
                    )
                to_lanes = pl.ds(
                    pl.multiple_of(c * main_cols + j * fold_cols, 128), fold_cols
                )
                rsend[d, :, to_lanes] = block.astype(BF16)

    def scatter(c):
        at_lanes = pl.ds(pl.multiple_of(c * main_cols, 128), main_cols)
        for k in range(1, devs):
            p = peer(k)
            remote(
                rsend.at[p, :, at_lanes],
                rrecv.at[me, :, at_lanes],
                rs_sem.at[0],
                rr_sem.at[c],
                p,
                s,
            ).start()
        rrecv[me, :, at_lanes] = rsend[me, :, at_lanes]

    for c in range(2):
        await_group(jnp.int32(c))
        dsend[c] = down(c, mate).astype(BF16)
        to_mate(c)
    kept_v[0] = down(0, s)

    def down_step(c, carry):
        from_mate(c - 1)
        await_group(c + 1)
        dsend[c + 1] = down(c + 1, mate).astype(BF16)
        fold(c - 1)
        to_mate(c + 1)
        scatter(c - 1)
        kept_v[lax.rem(c, 2)] = down(c, s)
        return carry

    lax.fori_loop(1, steps - 1, down_step, 0)
    from_mate(steps - 2)
    kept_v[(steps - 1) % 2] = down(steps - 1, s)
    fold(jnp.int32(steps - 2))
    scatter(steps - 2)
    from_mate(steps - 1)
    fold(jnp.int32(steps - 1))
    scatter(steps - 1)
    logits = logit_v[...] * inverse
    label = lax.broadcasted_iota(jnp.int32, (all_rows, count), 1)
    a = jnp.sum(jnp.where(label == e0, logits, 0.0), axis=-1, keepdims=True)
    b = jnp.sum(jnp.where(label == e1, logits, 0.0), axis=-1, keepdims=True)
    lead = jax.nn.sigmoid(a - b)
    pair_recv[:, :128] = lead + jnp.zeros((all_rows, 128), F32)
    my_rows = pl.ds(pl.multiple_of(me * rows, rows), rows)
    leading = pair_recv[my_rows, :128][:, 0:1]
    for b in range(devs * subs):
        pair_recv[...] = res_all[b].astype(F32)
        residual[:, b * part : (b + 1) * part] = pair_recv[my_rows, :]

    for copy in sends:
        copy.wait_send()
    for k in range(1, devs):
        block = res_all.at[block_of(me)]
        remote(block, block, fsend_sem.at[k], frecv_sem.at[me], me, mate).wait_send()
    remote(dsend, drecv, xsend_sem.at[0], xrecv_sem.at[0], me, mate).wait_send()

    for n in range(steps):
        least, end = n, n + 1
        others = rrecv.at[pl.ds(0, devs - 1), :, least * main_cols : end * main_cols]
        remote(others, others, rs_sem.at[0], rr_sem.at[n], beside, s).wait_recv()
        for c in range(least, end):
            from_lane = c * main_cols
            got = jnp.concatenate(
                [
                    rrecv[d, :, from_lane : from_lane + main_cols].astype(F32)
                    for d in range(devs)
                ],
                axis=0,
            ).astype(BF16)
            kept = jnp.dot(pick_v[0], got, preferred_element_type=F32)
            rest = jnp.zeros((2 * rows, fold_cols), F32)
            for j in range(folds):
                rest = rest + jnp.dot(
                    pick_v[1 + j],
                    got[:, j * fold_cols : (j + 1) * fold_cols],
                    preferred_element_type=F32,
                )
            both = jnp.concatenate([kept, rest], axis=1)
            at_cols = pl.ds(pl.multiple_of((2 * c + s) * CHUNK, CHUNK), CHUNK)
            mixture[:, at_cols] = leading * both[:rows] + (1.0 - leading) * both[rows:]
            swap = mixture.at[:, at_cols]
            remote(swap, swap, msend_sem.at[0], mrecv_sem.at[0], me, mate).start()

    others = rsend.at[pl.ds(0, devs - 1)]
    remote(others, others, rs_sem.at[0], rr_sem.at[0], beside, s).wait_send()
    swapped = mixture.at[:, pl.ds(0, width // 2)]
    remote(swapped, swapped, msend_sem.at[0], mrecv_sem.at[0], me, mate).wait()


def add_kernel(residual, mixture, layer_out, mixture_out):
    mixture_out[...] = mixture[...]
    layer_out[...] = (residual[...] + mixture[...]).astype(BF16)


def fits(mesh, shapes):
    devs, subs = mesh.shape["dev"], mesh.shape["sub"]
    hidden, query, keys, out_proj, router, gate_w, low_factor = shapes
    width = hidden[1]
    units = gate_w[1]
    cols = out_proj[1]
    return (
        subs == 2
        and devs == 4 * NEAR
        and devs * hidden[0] <= 128
        and hidden[0] == 8
        and CAP % (hidden[0] - CAP) == 0
        and CHUNK * CAP // hidden[0] % 128 == 0
        and CHUNK * CAP // hidden[0] == CAP // (hidden[0] - CAP) * (CHUNK - CHUNK * CAP // hidden[0])
        and query[2] == 128
        and cols % (128 * subs) == 0
        and cols * devs == width
        and low_factor[0] % cols == 0
        and units % CHUNK == 0
        and width % (2 * CHUNK) == 0
        and width // (2 * CHUNK) > 2
        and width // CHUNK % 2 == 0
        and devs % router[1] == 0
        and cols % (16 * SPLIT) == 0
        and units % (cols // SPLIT) == 0
        and width % units == 0
        and units % (2 * CHUNK) == 0
        and GATE_SLOTS * cols * units * 2 <= 48 * 10**6
        and GATE_SLOTS < 2 * devs
        and width // units * (units // (cols // SPLIT)) <= (2 * GATE_SLOTS - 2 * devs) * SPLIT
    )


def body(mesh, *args):
    (
        hidden,
        query,
        keys,
        values,
        lengths,
        out_proj,
        gain,
        router,
        low_factor,
        gate_w,
        up_w,
        down_w,
        gate_low,
        up_low,
        experts,
    ) = args
    shapes = [x.shape for x in (hidden, query, keys, out_proj, router, gate_w, low_factor)]
    if not fits(mesh, shapes):
        return plain_body(*args)
    devs, subs = mesh.shape["dev"], mesh.shape["sub"]
    rows, width = hidden.shape
    all_rows = devs * rows
    heads, hd = query.shape[1:]
    cols = out_proj.shape[1]
    part = cols // subs
    units = gate_w.shape[1]
    half, rank = low_factor.shape
    steps = width // (2 * CHUNK)
    anywhere = pl.BlockSpec(memory_space=pl.ANY)
    vmem = pl.BlockSpec(memory_space=pltpu.VMEM)
    smem = pl.BlockSpec(memory_space=pltpu.SMEM)
    dma = pltpu.SemaphoreType.DMA
    scratch = [
        pltpu.VMEM((GATE_SLOTS * cols, units), BF16),
        pltpu.VMEM((1, width), F32),
        pltpu.VMEM((router.shape[1], width), BF16),
        pltpu.VMEM(hidden.shape, BF16),
        pltpu.VMEM(query.shape, BF16),
        pltpu.VMEM(keys.shape, BF16),
        pltpu.VMEM(values.shape, BF16),
        pltpu.VMEM(out_proj.shape, BF16),
        pltpu.VMEM((subs, half, rank), BF16),
        pltpu.VMEM(gate_low.shape, BF16),
        pltpu.VMEM(up_low.shape, BF16),
        pltpu.VMEM((heads, rows, hd), F32),
        pltpu.VMEM((devs, rows, heads * hd + 128), BF16),
        pltpu.VMEM((devs, rows, part), BF16),
        pltpu.VMEM((all_rows, part), F32),
        pltpu.VMEM((all_rows, part), F32),
        pltpu.VMEM((devs * subs, all_rows, part), BF16),
        pltpu.VMEM((all_rows, cols), BF16),
        pltpu.VMEM((all_rows, 128), F32),
        pltpu.VMEM((all_rows, rank), F32),
        pltpu.VMEM((all_rows, router.shape[1]), F32),
        pltpu.VMEM((2, all_rows, units), F32),
        pltpu.VMEM((all_rows, units), BF16),
        pltpu.VMEM((steps, all_rows, CHUNK), BF16),
        pltpu.VMEM((steps, all_rows, CHUNK), BF16),
        pltpu.VMEM((2, all_rows, CHUNK), F32),
        pltpu.VMEM((devs, rows, steps * CHUNK * CAP // rows), BF16),
        pltpu.VMEM((devs, rows, steps * CHUNK * CAP // rows), BF16),
        pltpu.VMEM((all_rows, all_rows), BF16),
        pltpu.VMEM((1 + CAP // (rows - CAP), 2 * rows, all_rows), BF16),
        dma((10,)),
        dma((GATE_SLOTS,)),
        dma((width // units,)),
    ]
    scratch += [dma((devs,)) for _ in range(8)]
    scratch += [dma((2,)), dma((2,)), dma((1,)), dma((steps,))]
    scratch += [dma((1,)), dma((steps,)), dma((1,)), dma((1,))]
    residual, mixture = pl.pallas_call(
        functools.partial(layer_kernel, devs, subs, GATE_SLOTS),
        out_shape=(
            jax.ShapeDtypeStruct((rows, width), F32),
            jax.ShapeDtypeStruct((rows, width), F32),
        ),
        in_specs=[anywhere] * 4
        + [smem]
        + [anywhere] * 9
        + [smem],
        out_specs=(vmem, vmem),
        scratch_shapes=scratch,
        compiler_params=pltpu.CompilerParams(
            collective_id=0, has_side_effects=True, vmem_limit_bytes=VMEM_BYTES
        ),
    )(
        hidden,
        query,
        keys,
        values,
        lengths,
        out_proj,
        gain.reshape(1, width),
        router.T,
        low_factor,
        gate_w,
        up_w,
        down_w,
        gate_low,
        up_low,
        experts.T,
    )
    return pl.pallas_call(
        add_kernel,
        out_shape=(
            jax.ShapeDtypeStruct((rows, width), BF16),
            jax.ShapeDtypeStruct((rows, width), F32),
        ),
        in_specs=[vmem, vmem],
        out_specs=(vmem, vmem),
    )(residual, mixture)


def solution(mesh):
    placed = (
        P(("groups", "dev"), None),
        P(("groups", "dev"), "sub", None),
        P(("groups", "dev"), "sub", None, None),
        P(("groups", "dev"), "sub", None, None),
        P(("groups", "dev")),
        P("sub", "dev"),
        P(),
        P(),
        P("sub", None),
        P(None, ("dev", "sub")),
        P(None, ("dev", "sub")),
        P(("dev", "sub"), None),
        P(None, ("dev", "sub")),
        P(None, ("dev", "sub")),
        P(("groups", "dev"), None),
    )
    return jax.shard_map(
        functools.partial(body, mesh),
        mesh=mesh,
        in_specs=placed,
        out_specs=(P(("groups", "dev"), None), P(("groups", "dev"), None)),
        check_vma=False,
    )
```
